32 devices in a mesh: blk: 4 (over y, x), uly: 8 (over z, core).
Axes of the slice: x: 2, y: 2, z: 4, core: 2. Of those that a mesh axis runs over, the one named last changes fastest.
Arguments:
- query_proj: bfloat16 [2048, 1024], P(('blk', 'uly')), may hold values from -8 to 8
- key_proj: bfloat16 [2048, 1024], P(('blk', 'uly')), may hold values from -8 to 8
- value_proj: bfloat16 [2048, 1024], P(('blk', 'uly')), may hold values from -6 to 6
- attn_output: bfloat16 [2048, 1024], P(('blk', 'uly')), may hold values from -6 to 6
- out_grad: bfloat16 [2048, 1024], P(('blk', 'uly')), may hold values from -6 to 6
- random_blocks: int32 [16, 3], replicated, may hold values from 0 to 14, as said below
Outputs:
- query_grad: bfloat16 [2048, 1024], P(('blk', 'uly'))
- key_grad: bfloat16 [2048, 1024], P(('blk', 'uly'))
- value_grad: bfloat16 [2048, 1024], P(('blk', 'uly'))
The draws below stay inside these ranges and needn't reach their ends.
Inputs may be any that keep to these rules, and one draw needn't show every extreme that they name: `random_blocks`: every entry of row i names a block below i; row 0 names only block 0. The rows of one shard of blk (4 rows in a row, aligned) name at most 2 distinct blocks that lie in any one other shard, exactly 2 that lie in the shard just before theirs, and the rows of the last shard name exactly 2 that lie in the first shard.
All inputs are finite; a program needn't handle non-finite values.
Results may differ from the reference program's by a relative error of at most 0.005.
Values may be sent and summed in bfloat16 or wider, within the bound.
A program may use at most 64 MiB of HBM per device.

```python
import jax
import jax.numpy as jnp
from jax import lax

HD = 128
HEADS = 8
D = 1024
BLOCK = 128
RAND = 3
CAP = 2
SHARD = 512
SEQ = 2048
NB = 16


def pair_fields(key):
    base = jax.random.fold_in(key, 1234)
    draw_one, draw_two = jax.random.split(base, 2)
    full_width = HEADS * HD
    queries = jnp.clip(jax.random.normal(draw_one, (SEQ, full_width), jnp.float32), -4.0, 4.0)
    keys_drawn = jnp.clip(jax.random.normal(draw_two, (SEQ, full_width), jnp.float32), -4.0, 4.0)
    return (queries, keys_drawn)


def draw_query_proj(key, part):
    return pair_fields(key)[0].astype(jnp.bfloat16)


def draw_key_proj(key, part):
    return pair_fields(key)[1].astype(jnp.bfloat16)


def draw_random_blocks(key, part):
    per_shard = SHARD // BLOCK
    shard_count = NB // per_shard
    keys_all = jax.random.split(jax.random.fold_in(key, 77), 5)
    offsets = jax.random.randint(keys_all[0], (shard_count, shard_count), 0, per_shard, dtype=jnp.int32)
    block_ids = jnp.arange(NB, dtype=jnp.int32)
    shard_of = block_ids // per_shard
    local_of = block_ids % per_shard
    coin = jax.random.randint(keys_all[1], (NB, RAND), 0, 2, dtype=jnp.int32)
    source = jax.random.randint(keys_all[2], (NB, RAND), 0, jnp.maximum(shard_of, 1)[:, None], dtype=jnp.int32)
    slot = jax.random.randint(keys_all[3], (NB, RAND), 0, CAP, dtype=jnp.int32)
    local_pick = jax.random.randint(keys_all[4], (NB, RAND), 0, jnp.maximum(local_of, 1)[:, None], dtype=jnp.int32) + (shard_of * per_shard)[:, None]
    pool_offset = offsets[shard_of[:, None], source]
    remote_block = source * per_shard + (pool_offset + slot) % per_shard
    use_remote = (shard_of[:, None] >= 1) & ((local_of[:, None] == 0) | (coin == 1))
    entries = jnp.where(use_remote, remote_block, jnp.where(local_of[:, None] >= 1, local_pick, 0))
    previous = jnp.maximum(shard_of - 1, 0)
    forced = previous * per_shard + (offsets[shard_of, previous] + local_of) % per_shard
    force_here = (shard_of >= 1) & (local_of < CAP)
    entries = entries.at[:, 0].set(jnp.where(force_here, forced, entries[:, 0]))
    first_forced = (offsets[shard_of, 0] + local_of) % per_shard
    force_first = (shard_of == shard_count - 1) & (local_of < CAP)
    entries = entries.at[:, 1].set(jnp.where(force_first, first_forced, entries[:, 1]))
    entries = entries.at[NB - 1, RAND - 1].set(NB - 2)
    return entries.astype(jnp.int32)


def steps_of(key, shape, shards, smallest, top_value):
    def one(axis_at, parts):
        heights = jax.random.uniform(jax.random.fold_in(jax.random.fold_in(key, 6), axis_at), (parts,), jnp.float32, smallest / len(shards), top_value / len(shards))
        return jnp.repeat(jnp.exp(heights), shape[axis_at] // parts).reshape((-1,) + (1,) * (len(shape) - axis_at - 1))

    level = one(*shards[0])
    for cut in shards[1:]:
        level = level * one(*cut)
    return level


def noise(own_key, dims, width, limit, pieces=(), held_as=jnp.bfloat16):
    level = steps_of(own_key, dims, pieces, -0.22, 0.18) if pieces else 1.0
    result = jax.random.normal(own_key, dims, jnp.float32) * width * level
    return jnp.minimum(jnp.maximum(result, -limit), limit).astype(held_as)


def setup_inputs(seed: int = 0) -> dict:
    key_of = jax.random.split(jax.random.key(seed), 7)
    query_proj = draw_query_proj(jax.random.fold_in(key_of[6], 71), 0)
    key_proj = draw_key_proj(jax.random.fold_in(key_of[6], 71), 0)
    value_proj = noise(key_of[2], (SEQ, D), 1.0, 6.0, ((0, 32),))
    attn_output = noise(key_of[3], (SEQ, D), 1.0, 6.0, ((0, 32),))
    out_grad = noise(key_of[4], (SEQ, D), 1.0, 6.0, ((0, 32),))
    random_blocks = draw_random_blocks(jax.random.fold_in(key_of[6], 71), 0)
    return dict(query_proj=query_proj, key_proj=key_proj, value_proj=value_proj, attn_output=attn_output, out_grad=out_grad, random_blocks=random_blocks)


def head_grads(tensors, random_blocks):
    query_rows, key_rows, value_rows, output_rows, grad_rows = tensors
    score_scale = HD ** -0.5
    extent = 3 + RAND
    query_blocks = query_rows.reshape(NB, BLOCK, HD)
    key_blocks = key_rows.reshape(NB, BLOCK, HD)
    value_blocks = value_rows.reshape(NB, BLOCK, HD)
    grad_blocks = grad_rows.reshape(NB, BLOCK, HD)
    row_delta = jnp.sum(output_rows.astype(jnp.float32) * grad_rows.astype(jnp.float32), axis=1).reshape(NB, BLOCK)
    block_ids = jnp.arange(NB, dtype=jnp.int32)
    listed = jnp.concatenate([block_ids[:, None], block_ids[:, None] - 1, jnp.zeros((NB, 1), jnp.int32), random_blocks.astype(jnp.int32)], axis=1)
    order = jnp.arange(extent, dtype=jnp.int32)
    earlier = order[None, :] < order[:, None]
    repeated = jnp.any((listed[:, :, None] == listed[:, None, :]) & earlier[None, :, :], axis=2)
    usable = (listed >= 0) & jnp.logical_not(repeated)
    within = jnp.arange(BLOCK, dtype=jnp.int32)

    def visit(accum, block):
        key_acc, value_acc = accum
        safe = jnp.maximum(listed[block], 0)
        keep = usable[block]
        key_sel = key_blocks[safe].reshape(extent * BLOCK, HD)
        value_sel = value_blocks[safe].reshape(extent * BLOCK, HD)
        query_blk = query_blocks[block]
        grad_blk = grad_blocks[block]
        scores = jnp.dot(query_blk, key_sel.T, preferred_element_type=jnp.float32) * score_scale
        query_pos = block * BLOCK + within
        key_pos = (safe[:, None] * BLOCK + within[None, :]).reshape(-1)
        allowed = jnp.repeat(keep, BLOCK)[None, :] & (key_pos[None, :] <= query_pos[:, None])
        row_max = jnp.max(jnp.where(allowed, scores, -1e30), axis=1)
        total = jnp.sum(jnp.where(allowed, jnp.exp(scores - row_max[:, None]), 0.0), axis=1)
        log_total = row_max + jnp.log(total)
        probs = jnp.where(allowed, jnp.exp(scores - log_total[:, None]), 0.0)
        prob_grad = jnp.dot(grad_blk, value_sel.T, preferred_element_type=jnp.float32)
        score_grad = (probs * (prob_grad - row_delta[block][:, None]) * score_scale).astype(jnp.bfloat16)
        query_part = jnp.dot(score_grad, key_sel, preferred_element_type=jnp.float32).astype(jnp.bfloat16)
        key_part = jnp.dot(score_grad.T, query_blk, preferred_element_type=jnp.float32).reshape(extent, BLOCK, HD)
        value_part = jnp.dot(probs.astype(jnp.bfloat16).T, grad_blk, preferred_element_type=jnp.float32).reshape(extent, BLOCK, HD)
        return (key_acc.at[safe].add(key_part), value_acc.at[safe].add(value_part)), query_part

    zeros_acc = jnp.zeros((NB, BLOCK, HD), jnp.float32)
    (key_acc, value_acc), query_parts = lax.scan(visit, (zeros_acc, zeros_acc), block_ids)
    return (query_parts.reshape(SEQ, HD), key_acc.reshape(SEQ, HD).astype(jnp.bfloat16), value_acc.reshape(SEQ, HD).astype(jnp.bfloat16))


def split_heads(tensor):
    return tensor.reshape(SEQ, HEADS, HD).transpose(1, 0, 2)


def join_heads(tensor):
    return tensor.transpose(1, 0, 2).reshape(SEQ, HEADS * HD)


def reference(query_proj, key_proj, value_proj, attn_output, out_grad, random_blocks):
    stacked = (split_heads(query_proj), split_heads(key_proj), split_heads(value_proj), split_heads(attn_output), split_heads(out_grad))

    def per_head(tensors):
        return head_grads(tensors, random_blocks)

    query_grad, key_grad, value_grad = lax.map(per_head, stacked)
    return join_heads(query_grad), join_heads(key_grad), join_heads(value_grad)
```

```python
import functools
import math

import jax
import jax.numpy as jnp
from jax import lax
from jax.experimental import pallas as pl
from jax.experimental.pallas import tpu as pltpu
from jax.sharding import PartitionSpec as P

HD = 128
BLOCK = 128
RAND = 3
CAP = 2


def named_table(random_blocks, per_shard):
    block_count = random_blocks.shape[0]
    shard_count = block_count // per_shard
    entries = random_blocks.reshape(shard_count, per_shard * RAND)
    block_ids = jnp.arange(block_count, dtype=jnp.int32)
    named = jnp.any(entries[:, :, None] == block_ids[None, None, :], axis=1)
    owner = block_ids // per_shard
    named = named & (owner[None, :] != jnp.arange(shard_count, dtype=jnp.int32)[:, None])
    grouped = named.reshape(shard_count, shard_count, per_shard).astype(jnp.int32)
    rank_in = jnp.cumsum(grouped, axis=2) - grouped
    return (grouped, rank_in)


def send_slots(grouped, rank_in, cycle_rank, per_shard):
    mine = lax.dynamic_index_in_dim(grouped, cycle_rank, 1, keepdims=False)
    mine_rank = lax.dynamic_index_in_dim(rank_in, cycle_rank, 1, keepdims=False)
    slot_ids = jnp.arange(CAP, dtype=jnp.int32)
    hit = (mine[:, None, :] == 1) & (mine_rank[:, None, :] == slot_ids[None, :, None])
    positions = jnp.arange(per_shard, dtype=jnp.int32)
    select = jnp.sum(jnp.where(hit, positions[None, None, :], 0), axis=2)
    filled = jnp.any(hit, axis=2)
    return (select, filled)


def on_device(query_proj, key_proj, value_proj, attn_output, out_grad, random_blocks):
    tok_count = query_proj.shape[0]
    head_count = query_proj.shape[1] // HD
    score_scale = HD ** (-0.5)
    extent = 3 + RAND

    def to_heads(tensor):
        return tensor.reshape(tok_count, head_count, HD)

    query_rows, key_rows, value_rows, output_rows, grad_rows = (
        lax.all_to_all(to_heads(query_proj), "uly", split_axis=1, concat_axis=0, tiled=True),
        lax.all_to_all(to_heads(key_proj), "uly", split_axis=1, concat_axis=0, tiled=True),
        lax.all_to_all(to_heads(value_proj), "uly", split_axis=1, concat_axis=0, tiled=True),
        lax.all_to_all(to_heads(attn_output), "uly", split_axis=1, concat_axis=0, tiled=True),
        lax.all_to_all(to_heads(out_grad), "uly", split_axis=1, concat_axis=0, tiled=True),
    )
    row_delta = jnp.sum(
        output_rows.astype(jnp.float32) * grad_rows.astype(jnp.float32), axis=2
    ).reshape(-1)
    shard_len = query_rows.shape[0]
    per_shard = shard_len // BLOCK
    query_blocks = query_rows.reshape(per_shard, BLOCK, HD)
    key_blocks = key_rows.reshape(per_shard, BLOCK, HD)
    value_blocks = value_rows.reshape(per_shard, BLOCK, HD)
    grad_blocks = grad_rows.reshape(per_shard, BLOCK, HD)
    delta_blocks = row_delta.reshape(per_shard, BLOCK)
    cycle_size = lax.axis_size("blk")
    cycle_rank = lax.axis_index("blk")
    block_count = random_blocks.shape[0]
    grouped, rank_in = named_table(random_blocks, per_shard)
    select, filled = send_slots(grouped, rank_in, cycle_rank, per_shard)
    key_send = jnp.where(
        filled[:, :, None, None],
        jnp.take(key_blocks, select.reshape(-1), axis=0).reshape(cycle_size, CAP, BLOCK, HD),
        jnp.zeros((), jnp.bfloat16),
    )
    value_send = jnp.where(
        filled[:, :, None, None],
        jnp.take(value_blocks, select.reshape(-1), axis=0).reshape(cycle_size, CAP, BLOCK, HD),
        jnp.zeros((), jnp.bfloat16),
    )
    extra_key = jnp.broadcast_to(
        jnp.stack([key_blocks[per_shard - 1], key_blocks[0]])[None], (cycle_size, 2, BLOCK, HD)
    )
    extra_value = jnp.broadcast_to(
        jnp.stack([value_blocks[per_shard - 1], value_blocks[0]])[None], (cycle_size, 2, BLOCK, HD)
    )
    all_key, all_value = (
        lax.all_to_all(
            jnp.concatenate([key_send, extra_key], axis=1),
            "blk",
            split_axis=0,
            concat_axis=0,
            tiled=True,
        ),
        lax.all_to_all(
            jnp.concatenate([value_send, extra_value], axis=1),
            "blk",
            split_axis=0,
            concat_axis=0,
            tiled=True,
        ),
    )
    far_key = all_key[:, :CAP]
    far_value = all_value[:, :CAP]
    before_rank = jnp.maximum(cycle_rank - 1, 0)
    prev_key = lax.dynamic_index_in_dim(all_key, before_rank, 0, keepdims=False)[CAP]
    prev_value = lax.dynamic_index_in_dim(all_value, before_rank, 0, keepdims=False)[CAP]
    first_key = all_key[0, CAP + 1]
    first_value = all_value[0, CAP + 1]
    key_store = jnp.concatenate(
        [key_blocks, prev_key[None], first_key[None], far_key.reshape(cycle_size * CAP, BLOCK, HD)],
        axis=0,
    )
    value_store = jnp.concatenate(
        [
            value_blocks,
            prev_value[None],
            first_value[None],
            far_value.reshape(cycle_size * CAP, BLOCK, HD),
        ],
        axis=0,
    )
    store_size = key_store.shape[0]
    picked = lax.dynamic_slice_in_dim(random_blocks, cycle_rank * per_shard, per_shard, 0)
    own_rank = lax.dynamic_index_in_dim(rank_in, cycle_rank, 0, keepdims=False).reshape(-1)
    all_ids = jnp.arange(block_count, dtype=jnp.int32)
    slot_of = jnp.sum(
        jnp.where(picked[:, :, None] == all_ids[None, None, :], own_rank[None, None, :], 0), axis=2
    )
    owner = picked // per_shard
    random_index = jnp.where(
        owner == cycle_rank, picked - cycle_rank * per_shard, per_shard + 2 + owner * CAP + slot_of
    )
    local_ids = jnp.arange(per_shard, dtype=jnp.int32)
    global_ids = cycle_rank * per_shard + local_ids
    listed = jnp.concatenate(
        [
            global_ids[:, None],
            global_ids[:, None] - 1,
            jnp.zeros((per_shard, 1), jnp.int32),
            picked,
        ],
        axis=1,
    )
    first_index = jnp.zeros((per_shard, 1), jnp.int32) + jnp.where(
        cycle_rank == 0, 0, per_shard + 1
    ).astype(jnp.int32)
    store_index = jnp.concatenate(
        [
            local_ids[:, None],
            jnp.where(local_ids >= 1, local_ids - 1, per_shard)[:, None],
            first_index,
            random_index,
        ],
        axis=1,
    )
    order = jnp.arange(extent, dtype=jnp.int32)
    earlier = order[None, :] < order[:, None]
    repeated = jnp.any((listed[:, :, None] == listed[:, None, :]) & earlier[None, :, :], axis=2)
    usable = (listed >= 0) & jnp.logical_not(repeated)
    within = jnp.arange(BLOCK, dtype=jnp.int32)
    group = math.gcd(per_shard, max(1, 512 // BLOCK))
    group_count = per_shard // group

    def group_turn(carry, group_index):
        key_grad_store, value_grad_store = carry
        first = group_index * group
        query_grp = lax.dynamic_slice_in_dim(query_blocks, first, group, 0)
        grad_grp = lax.dynamic_slice_in_dim(grad_blocks, first, group, 0)
        delta_grp = lax.dynamic_slice_in_dim(delta_blocks, first, group, 0)
        index_grp = lax.dynamic_slice_in_dim(store_index, first, group, 0).reshape(-1)
        listed_grp = lax.dynamic_slice_in_dim(listed, first, group, 0)
        usable_grp = lax.dynamic_slice_in_dim(usable, first, group, 0)
        key_sel = jnp.take(key_store, index_grp, axis=0).reshape(group, extent * BLOCK, HD)
        value_sel = jnp.take(value_store, index_grp, axis=0).reshape(group, extent * BLOCK, HD)
        scores = (
            jnp.einsum("gqd,gkd->gqk", query_grp, key_sel, preferred_element_type=jnp.float32)
            * score_scale
        )
        query_pos = (cycle_rank * per_shard + first + jnp.arange(group, dtype=jnp.int32))[
            :, None
        ] * BLOCK + within[None, :]
        key_pos = (listed_grp[:, :, None] * BLOCK + within[None, None, :]).reshape(
            group, extent * BLOCK
        )
        allowed = jnp.repeat(usable_grp, BLOCK, axis=1)[:, None, :] & (
            key_pos[:, None, :] <= query_pos[:, :, None]
        )
        row_max = jnp.max(jnp.where(allowed, scores, -1e30), axis=2)
        total = jnp.sum(jnp.where(allowed, jnp.exp(scores - row_max[:, :, None]), 0.0), axis=2)
        log_total = row_max + jnp.log(total)
        probs = jnp.where(allowed, jnp.exp(scores - log_total[:, :, None]), 0.0)
        prob_grad = jnp.einsum(
            "gqd,gkd->gqk", grad_grp, value_sel, preferred_element_type=jnp.float32
        )
        score_grad = (probs * (prob_grad - delta_grp[:, :, None]) * score_scale).astype(
            jnp.bfloat16
        )
        query_part = jnp.einsum(
            "gqk,gkd->gqd", score_grad, key_sel, preferred_element_type=jnp.float32
        ).astype(jnp.bfloat16)
        key_part = jnp.einsum(
            "gqk,gqd->gkd", score_grad, query_grp, preferred_element_type=jnp.float32
        )
        value_part = jnp.einsum(
            "gqk,gqd->gkd", probs.astype(jnp.bfloat16), grad_grp, preferred_element_type=jnp.float32
        )
        key_grad_store = key_grad_store.at[index_grp].add(
            key_part.reshape(group * extent, BLOCK, HD)
        )
        value_grad_store = value_grad_store.at[index_grp].add(
            value_part.reshape(group * extent, BLOCK, HD)
        )
        return ((key_grad_store, value_grad_store), query_part)

    zero_store = jnp.zeros((store_size, BLOCK, HD), jnp.float32)
    (key_grad_store, value_grad_store), query_parts = lax.scan(
        group_turn, (zero_store, zero_store), jnp.arange(group_count, dtype=jnp.int32)
    )
    query_acc = query_parts.reshape(shard_len, HD)
    key_acc = key_grad_store[:per_shard]
    value_acc = value_grad_store[:per_shard]
    far_key_grad = key_grad_store[per_shard + 2 :].reshape(cycle_size, CAP, BLOCK, HD)
    far_value_grad = value_grad_store[per_shard + 2 :].reshape(cycle_size, CAP, BLOCK, HD)
    dest_ids = jnp.arange(cycle_size, dtype=jnp.int32)
    to_prev = (dest_ids == cycle_rank - 1)[:, None, None]
    to_first = (dest_ids == 0)[:, None, None]
    extra_key_grad = jnp.stack(
        [
            jnp.where(to_prev, key_grad_store[per_shard][None], 0.0),
            jnp.where(to_first, key_grad_store[per_shard + 1][None], 0.0),
        ],
        axis=1,
    )
    extra_value_grad = jnp.stack(
        [
            jnp.where(to_prev, value_grad_store[per_shard][None], 0.0),
            jnp.where(to_first, value_grad_store[per_shard + 1][None], 0.0),
        ],
        axis=1,
    )
    all_key_back, all_value_back = (
        lax.all_to_all(
            jnp.concatenate([far_key_grad, extra_key_grad], axis=1),
            "blk",
            split_axis=0,
            concat_axis=0,
            tiled=True,
        ),
        lax.all_to_all(
            jnp.concatenate([far_value_grad, extra_value_grad], axis=1),
            "blk",
            split_axis=0,
            concat_axis=0,
            tiled=True,
        ),
    )
    back_key = all_key_back[:, :CAP]
    back_value = all_value_back[:, :CAP]
    prev_back = jnp.stack(
        [jnp.sum(all_key_back[:, CAP], axis=0), jnp.sum(all_value_back[:, CAP], axis=0)]
    )
    first_back = jnp.stack(
        [jnp.sum(all_key_back[:, CAP + 1], axis=0), jnp.sum(all_value_back[:, CAP + 1], axis=0)]
    )
    key_acc = key_acc.at[per_shard - 1].add(prev_back[0]).at[0].add(first_back[0])
    value_acc = value_acc.at[per_shard - 1].add(prev_back[1]).at[0].add(first_back[1])
    back_key = jnp.where(filled[:, :, None, None], back_key, 0.0).reshape(
        cycle_size * CAP, BLOCK, HD
    )
    back_value = jnp.where(filled[:, :, None, None], back_value, 0.0).reshape(
        cycle_size * CAP, BLOCK, HD
    )
    key_acc = key_acc.at[select.reshape(-1)].add(back_key).reshape(shard_len, HD)
    value_acc = value_acc.at[select.reshape(-1)].add(back_value).reshape(shard_len, HD)
    outgoing = (
        query_acc.reshape(shard_len, 1, HD),
        key_acc.astype(jnp.bfloat16).reshape(shard_len, 1, HD),
        value_acc.astype(jnp.bfloat16).reshape(shard_len, 1, HD),
    )
    query_back, key_back, value_back = (
        lax.all_to_all(outgoing[0], "uly", split_axis=0, concat_axis=1, tiled=True),
        lax.all_to_all(outgoing[1], "uly", split_axis=0, concat_axis=1, tiled=True),
        lax.all_to_all(outgoing[2], "uly", split_axis=0, concat_axis=1, tiled=True),
    )
    return (
        query_back.reshape(tok_count, head_count * HD),
        key_back.reshape(tok_count, head_count * HD),
        value_back.reshape(tok_count, head_count * HD),
    )


NEG = -1e30
KEY, QUERY, GRAD, VALUE = 0, 1, 2, 3
D_QUERY, D_KEY, D_VALUE = 0, 1, 2
ROWS_BY_COLS = (((1,), (1,)), ((), ()))
COLS_BY_COLS = (((0,), (0,)), ((), ()))


def flip(value, mask, count):
    if count & (count - 1):
        return lax.rem(value + mask, count)
    for bit in range(count.bit_length() - 1):
        if mask >> bit & 1:
            value = value + (1 << bit) * (1 - 2 * (value // (1 << bit) % 2))
    return value


def core_of(shard):
    return (shard + 1) // 2 % 2


def fused_kernel(
    shards,
    uly,
    picks_hbm,
    q_ref,
    k_ref,
    v_ref,
    o_ref,
    g_ref,
    out_ref,
    picks_ref,
    rows_in,
    held,
    delta_send,
    delta_recv,
    bias,
    stats,
    scores,
    probs_low,
    score_grads,
    acc,
    partial,
    outgoing,
    zs,
    zr,
    sb,
    st,
    pt,
    ds_sem,
    dr_sem,
    os_sem,
    or_sem,
    il,
):
    tok = q_ref.shape[0]
    length = tok * uly
    per = length // BLOCK
    gp = BLOCK // tok
    blocks = per * shards
    planes = uly // shards
    base = (uly // 2 - planes) // 2
    scale = HD ** (-0.5)
    f32 = jnp.float32
    b = lax.axis_index("blk")
    u = lax.axis_index("uly")
    uz, core = u // 2, u % 2
    plane = uz - base
    is_home = jnp.logical_and(plane >= 0, plane < planes)
    near = jnp.clip(plane, 0, planes - 1)
    head = b + shards * near
    own_source = jnp.logical_and(is_home, core_of(b) == core)
    inputs = {KEY: k_ref, QUERY: q_ref, VALUE: v_ref, GRAD: g_ref}
    mesh_ids = pl.DeviceIdType.MESH

    def home(h, s):
        return h % shards, (base + h // shards) * 2 + core_of(s)

    sibling = (b, uz * 2 + 1 - core)

    def is_self(place):
        return jnp.logical_and(place[0] == b, place[1] == u)

    def ids(place):
        return {"blk": place[0], "uly": place[1]}

    def cols(p):
        return pl.ds(pl.multiple_of(p * HD, HD), HD)

    def rows(p):
        return pl.ds(pl.multiple_of(p * tok, tok), tok)

    def remote(source, target, send, recv, place):
        return pltpu.make_async_remote_copy(
            src_ref=source,
            dst_ref=target,
            send_sem=send,
            recv_sem=recv,
            device_id=ids(place),
            device_id_type=mesh_ids,
        )

    def ship(source, target, send, recv, place):
        mine = is_self(place)

        @pl.when(jnp.logical_not(mine))
        def _():
            remote(source, target, send, recv, place).start()

        @pl.when(mine)
        def _():
            pltpu.make_async_copy(source, target, recv).start()

    def heads():
        return [flip(head, mask, uly) for mask in reversed(range(uly))]

    def z_send(t):
        for h in heads():
            ship(
                inputs[t].at[:, cols(h)],
                held.at[t, b, rows(u), :],
                zs.at[0],
                zr.at[t, b // 2],
                home(h, b),
            )

    fetches = (
        pltpu.make_async_copy(o_ref, rows_in.at[0], il.at[0]),
        pltpu.make_async_copy(g_ref, rows_in.at[1], il.at[1]),
        pltpu.make_async_copy(picks_hbm, picks_ref, il.at[2]),
    )
    barrier = pltpu.get_barrier_semaphore()

    def greet(place):
        pl.semaphore_signal(barrier, inc=1, device_id=ids(place), device_id_type=mesh_ids)

    with jax.named_scope("greet"):

        @pl.when(is_home)
        def _():
            for j in range(shards // 2):
                s = 2 * j + (core + j) % 2
                for mask in reversed(range(uly)):
                    place = (s, flip(u, mask, uly))
                    pl.when(jnp.logical_not(is_self(place)))(functools.partial(greet, place))
            greet(sibling)

        for fetch in fetches:
            fetch.start()
    with jax.named_scope("barrier"):
        pl.semaphore_wait(
            barrier, uly - jnp.where(own_source, 1, 0) + jnp.where(is_home, 1, 0)
        )
    with jax.named_scope("send_kq"):
        z_send(KEY)
        z_send(QUERY)

    with jax.named_scope("prep"):
        for fetch in fetches:
            fetch.wait()
        product = rows_in[0].astype(f32) * rows_in[1].astype(f32)
        high = product.astype(jnp.bfloat16)
        low = (product - high.astype(f32)).astype(jnp.bfloat16)
        head_of = lax.broadcasted_iota(jnp.int32, (uly, uly * HD), 1) // HD
        pick_head = jnp.where(
            head_of == lax.broadcasted_iota(jnp.int32, (uly, uly * HD), 0), 1.0, 0.0
        ).astype(jnp.bfloat16)
        sums = sum(
            lax.dot_general(
                pick_head,
                jnp.concatenate([part] * gp, axis=0),
                ROWS_BY_COLS,
                preferred_element_type=f32,
            )
            for part in (high, low)
        )
        place_of = lax.broadcasted_iota(jnp.int32, (uly, BLOCK), 1) // tok
        sums = jnp.where(place_of == lax.rem(u, gp), sums, 0.0)
        for h in range(uly):
            delta_send[h] = sums[h : h + 1]

    with jax.named_scope("send_gv"):
        for h in heads():
            ship(
                delta_send.at[h], delta_recv.at[b // 2, u], ds_sem.at[0], dr_sem.at[0], home(h, b)
            )
        z_send(GRAD)
        z_send(VALUE)

    def at(jb):
        return pl.ds(jb * BLOCK, BLOCK)

    def run_home(c):
        owned = [s for s in range(shards) if core_of(s) == c]
        foreign = [s for s in range(shards) if core_of(s) != c and s > owned[0]]
        lent = [s for s in owned if any(core_of(k) != c and k < s for k in range(shards))]
        tiles = [(q, k) for k in owned for q in range(k, shards)]
        slot = {tile: n for n, tile in enumerate(tiles)}
        q_all = sorted({q for q, _ in tiles})
        q_own = [q for q in q_all if q in owned]
        q_far = [q for q in q_all if q not in owned]
        pair_of = {QUERY: 0, GRAD: 1}

        def own(t):
            with jax.named_scope(f"own_{t}"):
                for s in owned:
                    ref = held.at[t, s]
                    remote(ref, ref, zs.at[0], zr.at[t, s // 2], (b, u)).wait_recv()
                    if t in pair_of and s in lent:
                        sem = sb.at[pair_of[t], s]
                        remote(ref, ref, sem, sem, sibling).start()

        def lent_copy(t, s):
            sem = sb.at[pair_of[t], s]
            return remote(held.at[t, s], held.at[t, s], sem, sem, sibling)

        def tile_first(q, k, jb):
            return jb * BLOCK if q == k else 0

        def widen(row, first, fill):
            if first:
                return jnp.concatenate([jnp.full((1, first), fill, f32), row], axis=1)
            return row

        def make_scores(q, k, top):
            with jax.named_scope(f"scores_{q}_{k}"):
                for jb in range(per):
                    first = tile_first(q, k, jb)
                    tile = lax.dot_general(
                        held[KEY, k, at(jb), :],
                        held[QUERY, q, first:, :],
                        ROWS_BY_COLS,
                        preferred_element_type=f32,
                    )
                    tile = tile * scale + bias[q, pl.ds(k * per + jb, 1), first:]
                    if q == k:
                        wide = length - first
                        key_at = lax.broadcasted_iota(jnp.int32, (BLOCK, wide), 0)
                        query_at = lax.broadcasted_iota(jnp.int32, (BLOCK, wide), 1)
                        tile = jnp.where(key_at <= query_at, tile, NEG)
                    scores[slot[q, k], at(jb), first:] = tile
                    high = widen(jnp.max(tile, axis=0, keepdims=True), first, NEG)
                    top = high if top is None else jnp.maximum(top, high)
            return top

        def make_exps(q, top):
            with jax.named_scope(f"exps_{q}"):
                total = jnp.zeros((1, length), f32)
                for k in owned:
                    if k > q:
                        continue
                    for jb in range(per):
                        first = tile_first(q, k, jb)
                        tile = jnp.exp(scores[slot[q, k], at(jb), first:] - top[:, first:])
                        scores[slot[q, k], at(jb), first:] = tile
                        part = jnp.sum(tile, axis=0, keepdims=True)
                        total = total + widen(part, first, 0.0)
                stats[c, q, 0:1, :] = top
                stats[c, q, 1:2, :] = total

        def make_probs(q, k, factor):
            with jax.named_scope(f"probs_{q}_{k}"):
                for jb in range(per):
                    first = tile_first(q, k, jb)
                    probs = scores[slot[q, k], at(jb), first:] * factor[:, first:]
                    if first:
                        blank = jnp.zeros((BLOCK, first), jnp.bfloat16)
                        probs_low[slot[q, k], at(jb), :first] = blank
                    probs_low[slot[q, k], at(jb), first:] = probs.astype(jnp.bfloat16)

        def add(ref, value, fresh):
            if fresh:
                ref[...] = value
            else:
                ref[...] += value

        def make_values(q, k, fresh):
            with jax.named_scope(f"values_{q}_{k}"):
                product = jnp.dot(
                    probs_low[slot[q, k]], held[GRAD, q], preferred_element_type=f32
                )
                add(acc.at[D_VALUE, k], product, fresh)

        def make_grads(q, k, factor, delta):
            with jax.named_scope(f"grads_{q}_{k}"):
                for jb in range(per):
                    first = tile_first(q, k, jb)
                    prob_grad = lax.dot_general(
                        held[VALUE, k, at(jb), :],
                        held[GRAD, q, first:, :],
                        ROWS_BY_COLS,
                        preferred_element_type=f32,
                    )
                    grads = (scores[slot[q, k], at(jb), first:] * factor[:, first:]) * (
                        prob_grad - delta[:, first:]
                    )
                    if first:
                        score_grads[at(jb), :first] = jnp.zeros((BLOCK, first), jnp.bfloat16)
                    score_grads[at(jb), first:] = grads.astype(jnp.bfloat16)

        def add_query(q, k, fresh):
            product = lax.dot_general(
                score_grads[...], held[KEY, k], COLS_BY_COLS, preferred_element_type=f32
            )
            add(acc.at[D_QUERY, q], product, fresh)

        def add_key(q, k, fresh):
            product = jnp.dot(score_grads[...], held[QUERY, q], preferred_element_type=f32)
            add(acc.at[D_KEY, k], product, fresh)

        def send_result(t, s):
            with jax.named_scope(f"send_{t}_{s}"):
                outgoing[t, s // 2] = acc[t, s].astype(jnp.bfloat16)
                for mask in list(range(1, uly)) + [0]:
                    p = flip(u, mask, uly)
                    ship(
                        outgoing.at[t, s // 2, rows(p), :],
                        out_ref.at[t, :, cols(head)],
                        os_sem.at[0],
                        or_sem.at[0],
                        (s, p),
                    )

        own(KEY)
        own(QUERY)
        tops = {}
        for q in q_own:
            for k in owned:
                if k <= q:
                    tops[q] = make_scores(q, k, tops.get(q))
        for q in q_own:
            make_exps(q, tops[q])
        for q in q_far:
            with jax.named_scope("lent_q"):
                lent_copy(QUERY, q).wait_recv()
            for k in owned:
                if k <= q:
                    tops[q] = make_scores(q, k, tops.get(q))
            make_exps(q, tops[q])
        with jax.named_scope("stats"):
            remote(delta_recv, delta_recv, ds_sem.at[0], dr_sem.at[0], (b, u)).wait_recv()
            for s in owned:
                pieces = []
                for n in range(per):
                    piece = delta_recv[s // 2, n * gp]
                    for i in range(1, gp):
                        piece = piece + delta_recv[s // 2, n * gp + i]
                    pieces.append(piece)
                stats[c, s, 2:3, :] = jnp.concatenate(pieces, axis=1)
            remote(stats.at[c], stats.at[c], st.at[c], st.at[c], sibling).start()
        own(GRAD)
        with jax.named_scope("stats_wait"):
            remote(stats.at[1 - c], stats.at[1 - c], st.at[c], st.at[1 - c], sibling).wait_recv()
        factors, deltas = {}, {}
        for q in q_all:
            top, total = stats[c, q, 0:1, :], stats[c, q, 1:2, :]
            if any(core_of(k) != c for k in range(q + 1)):
                top_far, total_far = stats[1 - c, q, 0:1, :], stats[1 - c, q, 1:2, :]
                high = jnp.maximum(top, top_far)
                share = jnp.exp(top - high)
                factors[q] = share / (share * total + jnp.exp(top_far - high) * total_far)
            else:
                factors[q] = 1.0 / total
            deltas[q] = stats[c if q in owned else 1 - c, q, 2:3, :]
        for q, k in tiles:
            make_probs(q, k, factors[q])
        fresh = {}
        for q in q_own + q_far:
            if q in q_far:
                with jax.named_scope("lent_g"):
                    lent_copy(GRAD, q).wait_recv()
            for k in owned:
                if k <= q:
                    make_values(q, k, fresh.setdefault(("v", k), True))
                    fresh["v", k] = False
        for k in owned:
            send_result(D_VALUE, k)
        own(VALUE)
        for q in q_far + q_own:
            for k in owned:
                if k <= q:
                    make_grads(q, k, factors[q] * scale, deltas[q])
                    with jax.named_scope(f"dots_{q}_{k}"):
                        add_query(q, k, fresh.setdefault(("q", q), True))
                        add_key(q, k, fresh.setdefault(("k", k), True))
                    fresh["q", q] = fresh["k", k] = False
            if q in q_far:
                ref = acc.at[D_QUERY, q]
                remote(ref, partial.at[q], pt.at[q], pt.at[q], sibling).start()
        for k in owned:
            send_result(D_KEY, k)
        for q in owned:
            if q in lent:
                with jax.named_scope("partial"):
                    ref = partial.at[q]
                    remote(ref, ref, pt.at[q], pt.at[q], sibling).wait_recv()
                    acc[D_QUERY, q] += partial[q]
            send_result(D_QUERY, q)
        with jax.named_scope("lent_sent"):
            for s in lent:
                for t in pair_of:
                    lent_copy(t, s).wait_send()
            for q in q_far:
                ref = acc.at[D_QUERY, q]
                remote(ref, ref, pt.at[q], pt.at[q], sibling).wait_send()
            remote(stats.at[c], stats.at[c], st.at[c], st.at[c], sibling).wait_send()

    @pl.when(is_home)
    def _():
        with jax.named_scope("bias"):
            lane_block = lax.broadcasted_iota(jnp.int32, (1, length), 1) // BLOCK
            key_block = lax.broadcasted_iota(jnp.int32, (blocks, length), 0)
            for s in range(shards):
                query_block = lane_block + s * per
                hit = (key_block == query_block) | (key_block == query_block - 1)
                hit = hit | (key_block == 0)
                for r in range(RAND):
                    named = jnp.zeros((1, length), jnp.int32)
                    for i in range(per):
                        named = jnp.where(lane_block == i, picks_ref[r, s * per + i], named)
                    hit = hit | (key_block == named)
                hit = hit & (key_block <= query_block)
                bias[s] = jnp.where(hit, 0.0, NEG)
        for c in range(2):
            pl.when(core == c)(functools.partial(run_home, c))

    def drain(count):
        ref = held.at[:, 0, pl.ds(0, count * tok), :]
        remote(ref, ref, zs.at[0], zr.at[0, 0], (b, u)).wait_send()
        ref = delta_send.at[pl.ds(0, count)]
        remote(ref, ref, ds_sem.at[0], dr_sem.at[0], (b, u)).wait_send()

    with jax.named_scope("sent"):
        pl.when(own_source)(lambda: drain(uly - 1))
        pl.when(jnp.logical_not(own_source))(lambda: drain(uly))

        @pl.when(own_source)
        def _():
            ref = outgoing.at[:, :, pl.ds(0, length - tok // (shards // 2)), :]
            remote(ref, ref, os_sem.at[0], or_sem.at[0], (b, u)).wait_send()

        @pl.when(jnp.logical_and(is_home, jnp.logical_not(own_source)))
        def _():
            remote(outgoing, outgoing, os_sem.at[0], or_sem.at[0], (b, u)).wait_send()

    with jax.named_scope("landed"):
        remote(out_ref, out_ref, os_sem.at[0], or_sem.at[0], (b, u)).wait_recv()


def write_out(held, a_out, b_out, c_out, done):
    writes = [
        pltpu.make_async_copy(held.at[i], target, done.at[i])
        for i, target in enumerate((a_out, b_out, c_out))
    ]
    for write in writes:
        write.start()
    for write in writes:
        write.wait()


def fused_on_device(shards, uly, q, k, v, o, g, random_blocks):
    tok, width = q.shape
    length = tok * uly
    per = length // BLOCK
    half = shards // 2
    tiles = max(
        sum(shards - k for k in range(shards) if core_of(k) == core) for core in range(2)
    )
    dma = pltpu.SemaphoreType.DMA
    hbm = pl.BlockSpec(memory_space=pltpu.HBM)
    vmem = pl.BlockSpec(memory_space=pltpu.VMEM)
    placed = [
        pltpu.with_memory_space_constraint(x, pltpu.HBM) for x in (random_blocks.T, q, k, v, o, g)
    ]
    results = pl.pallas_call(
        functools.partial(fused_kernel, shards, uly),
        out_shape=jax.ShapeDtypeStruct((3, tok, width), jnp.bfloat16),
        in_specs=[hbm] * 6,
        out_specs=vmem,
        scratch_shapes=[
            pltpu.SMEM(random_blocks.shape[::-1], jnp.int32),
            pltpu.VMEM((2, tok, width), jnp.bfloat16),
            pltpu.VMEM((4, shards, length, HD), jnp.bfloat16),
            pltpu.VMEM((uly, 1, BLOCK), jnp.float32),
            pltpu.VMEM((half, uly, 1, BLOCK), jnp.float32),
            pltpu.VMEM((shards, shards * per, length), jnp.float32),
            pltpu.VMEM((2, shards, 3, length), jnp.float32),
            pltpu.VMEM((tiles, length, length), jnp.float32),
            pltpu.VMEM((tiles, length, length), jnp.bfloat16),
            pltpu.VMEM((length, length), jnp.bfloat16),
            pltpu.VMEM((3, shards, length, HD), jnp.float32),
            pltpu.VMEM((shards, length, HD), jnp.float32),
            pltpu.VMEM((3, half, length, HD), jnp.bfloat16),
            dma((1,)),
            dma((4, half)),
            dma((2, shards)),
            dma((2,)),
            dma((shards,)),
            dma((1,)),
            dma((1,)),
            dma((1,)),
            dma((1,)),
            dma((3,)),
        ],
        compiler_params=pltpu.CompilerParams(
            collective_id=0, has_side_effects=True, vmem_limit_bytes=32 * 1024 * 1024
        ),
    )(*placed)
    return pl.pallas_call(
        write_out,
        out_shape=[jax.ShapeDtypeStruct((tok, width), jnp.bfloat16)] * 3,
        in_specs=[vmem],
        out_specs=[hbm] * 3,
        scratch_shapes=[dma((3,))],
        compiler_params=pltpu.CompilerParams(vmem_limit_bytes=32 * 1024 * 1024),
    )(results)


def wide_or_fused(shards, uly, *operands):
    tok, width = operands[0].shape
    length = tok * uly
    fits = shards * length * length * 4 <= 4 * 1024 * 1024
    paired = shards % 4 == 0 and uly % shards == 0
    if fits and paired and width == uly * HD and BLOCK % tok == 0 and length % BLOCK == 0:
        return tuple(fused_on_device(shards, uly, *operands))
    return on_device(*operands)


def solution(mesh):
    return jax.shard_map(
        functools.partial(wide_or_fused, mesh.shape["blk"], mesh.shape["uly"]),
        mesh=mesh,
        in_specs=(
            P(("blk", "uly"), None),
            P(("blk", "uly"), None),
            P(("blk", "uly"), None),
            P(("blk", "uly"), None),
            P(("blk", "uly"), None),
            P(),
        ),
        out_specs=(P(("blk", "uly"), None), P(("blk", "uly"), None), P(("blk", "uly"), None)),
        check_vma=False,
    )
```

```python
import functools
import math

import jax
import jax.numpy as jnp
from jax import lax
from jax.experimental import pallas as pl
from jax.experimental.pallas import tpu as pltpu
from jax.sharding import PartitionSpec as P

HD = 128
BLOCK = 128
RAND = 3
CAP = 2


def named_table(random_blocks, per_shard):
    block_count = random_blocks.shape[0]
    shard_count = block_count // per_shard
    entries = random_blocks.reshape(shard_count, per_shard * RAND)
    block_ids = jnp.arange(block_count, dtype=jnp.int32)
    named = jnp.any(entries[:, :, None] == block_ids[None, None, :], axis=1)
    owner = block_ids // per_shard
    named = named & (owner[None, :] != jnp.arange(shard_count, dtype=jnp.int32)[:, None])
    grouped = named.reshape(shard_count, shard_count, per_shard).astype(jnp.int32)
    rank_in = jnp.cumsum(grouped, axis=2) - grouped
    return (grouped, rank_in)


def send_slots(grouped, rank_in, cycle_rank, per_shard):
    mine = lax.dynamic_index_in_dim(grouped, cycle_rank, 1, keepdims=False)
    mine_rank = lax.dynamic_index_in_dim(rank_in, cycle_rank, 1, keepdims=False)
    slot_ids = jnp.arange(CAP, dtype=jnp.int32)
    hit = (mine[:, None, :] == 1) & (mine_rank[:, None, :] == slot_ids[None, :, None])
    positions = jnp.arange(per_shard, dtype=jnp.int32)
    select = jnp.sum(jnp.where(hit, positions[None, None, :], 0), axis=2)
    filled = jnp.any(hit, axis=2)
    return (select, filled)


def on_device(query_proj, key_proj, value_proj, attn_output, out_grad, random_blocks):
    tok_count = query_proj.shape[0]
    head_count = query_proj.shape[1] // HD
    score_scale = HD ** (-0.5)
    extent = 3 + RAND

    def to_heads(tensor):
        return tensor.reshape(tok_count, head_count, HD)

    query_rows, key_rows, value_rows, output_rows, grad_rows = (
        lax.all_to_all(to_heads(query_proj), "uly", split_axis=1, concat_axis=0, tiled=True),
        lax.all_to_all(to_heads(key_proj), "uly", split_axis=1, concat_axis=0, tiled=True),
        lax.all_to_all(to_heads(value_proj), "uly", split_axis=1, concat_axis=0, tiled=True),
        lax.all_to_all(to_heads(attn_output), "uly", split_axis=1, concat_axis=0, tiled=True),
        lax.all_to_all(to_heads(out_grad), "uly", split_axis=1, concat_axis=0, tiled=True),
    )
    row_delta = jnp.sum(
        output_rows.astype(jnp.float32) * grad_rows.astype(jnp.float32), axis=2
    ).reshape(-1)
    shard_len = query_rows.shape[0]
    per_shard = shard_len // BLOCK
    query_blocks = query_rows.reshape(per_shard, BLOCK, HD)
    key_blocks = key_rows.reshape(per_shard, BLOCK, HD)
    value_blocks = value_rows.reshape(per_shard, BLOCK, HD)
    grad_blocks = grad_rows.reshape(per_shard, BLOCK, HD)
    delta_blocks = row_delta.reshape(per_shard, BLOCK)
    cycle_size = lax.axis_size("blk")
    cycle_rank = lax.axis_index("blk")
    block_count = random_blocks.shape[0]
    grouped, rank_in = named_table(random_blocks, per_shard)
    select, filled = send_slots(grouped, rank_in, cycle_rank, per_shard)
    key_send = jnp.where(
        filled[:, :, None, None],
        jnp.take(key_blocks, select.reshape(-1), axis=0).reshape(cycle_size, CAP, BLOCK, HD),
        jnp.zeros((), jnp.bfloat16),
    )
    value_send = jnp.where(
        filled[:, :, None, None],
        jnp.take(value_blocks, select.reshape(-1), axis=0).reshape(cycle_size, CAP, BLOCK, HD),
        jnp.zeros((), jnp.bfloat16),
    )
    extra_key = jnp.broadcast_to(
        jnp.stack([key_blocks[per_shard - 1], key_blocks[0]])[None], (cycle_size, 2, BLOCK, HD)
    )
    extra_value = jnp.broadcast_to(
        jnp.stack([value_blocks[per_shard - 1], value_blocks[0]])[None], (cycle_size, 2, BLOCK, HD)
    )
    all_key, all_value = (
        lax.all_to_all(
            jnp.concatenate([key_send, extra_key], axis=1),
            "blk",
            split_axis=0,
            concat_axis=0,
            tiled=True,
        ),
        lax.all_to_all(
            jnp.concatenate([value_send, extra_value], axis=1),
            "blk",
            split_axis=0,
            concat_axis=0,
            tiled=True,
        ),
    )
    far_key = all_key[:, :CAP]
    far_value = all_value[:, :CAP]
    before_rank = jnp.maximum(cycle_rank - 1, 0)
    prev_key = lax.dynamic_index_in_dim(all_key, before_rank, 0, keepdims=False)[CAP]
    prev_value = lax.dynamic_index_in_dim(all_value, before_rank, 0, keepdims=False)[CAP]
    first_key = all_key[0, CAP + 1]
    first_value = all_value[0, CAP + 1]
    key_store = jnp.concatenate(
        [key_blocks, prev_key[None], first_key[None], far_key.reshape(cycle_size * CAP, BLOCK, HD)],
        axis=0,
    )
    value_store = jnp.concatenate(
        [
            value_blocks,
            prev_value[None],
            first_value[None],
            far_value.reshape(cycle_size * CAP, BLOCK, HD),
        ],
        axis=0,
    )
    store_size = key_store.shape[0]
    picked = lax.dynamic_slice_in_dim(random_blocks, cycle_rank * per_shard, per_shard, 0)
    own_rank = lax.dynamic_index_in_dim(rank_in, cycle_rank, 0, keepdims=False).reshape(-1)
    all_ids = jnp.arange(block_count, dtype=jnp.int32)
    slot_of = jnp.sum(
        jnp.where(picked[:, :, None] == all_ids[None, None, :], own_rank[None, None, :], 0), axis=2
    )
    owner = picked // per_shard
    random_index = jnp.where(
        owner == cycle_rank, picked - cycle_rank * per_shard, per_shard + 2 + owner * CAP + slot_of
    )
    local_ids = jnp.arange(per_shard, dtype=jnp.int32)
    global_ids = cycle_rank * per_shard + local_ids
    listed = jnp.concatenate(
        [
            global_ids[:, None],
            global_ids[:, None] - 1,
            jnp.zeros((per_shard, 1), jnp.int32),
            picked,
        ],
        axis=1,
    )
    first_index = jnp.zeros((per_shard, 1), jnp.int32) + jnp.where(
        cycle_rank == 0, 0, per_shard + 1
    ).astype(jnp.int32)
    store_index = jnp.concatenate(
        [
            local_ids[:, None],
            jnp.where(local_ids >= 1, local_ids - 1, per_shard)[:, None],
            first_index,
            random_index,
        ],
        axis=1,
    )
    order = jnp.arange(extent, dtype=jnp.int32)
    earlier = order[None, :] < order[:, None]
    repeated = jnp.any((listed[:, :, None] == listed[:, None, :]) & earlier[None, :, :], axis=2)
    usable = (listed >= 0) & jnp.logical_not(repeated)
    within = jnp.arange(BLOCK, dtype=jnp.int32)
    group = math.gcd(per_shard, max(1, 512 // BLOCK))
    group_count = per_shard // group

    def group_turn(carry, group_index):
        key_grad_store, value_grad_store = carry
        first = group_index * group
        query_grp = lax.dynamic_slice_in_dim(query_blocks, first, group, 0)
        grad_grp = lax.dynamic_slice_in_dim(grad_blocks, first, group, 0)
        delta_grp = lax.dynamic_slice_in_dim(delta_blocks, first, group, 0)
        index_grp = lax.dynamic_slice_in_dim(store_index, first, group, 0).reshape(-1)
        listed_grp = lax.dynamic_slice_in_dim(listed, first, group, 0)
        usable_grp = lax.dynamic_slice_in_dim(usable, first, group, 0)
        key_sel = jnp.take(key_store, index_grp, axis=0).reshape(group, extent * BLOCK, HD)
        value_sel = jnp.take(value_store, index_grp, axis=0).reshape(group, extent * BLOCK, HD)
        scores = (
            jnp.einsum("gqd,gkd->gqk", query_grp, key_sel, preferred_element_type=jnp.float32)
            * score_scale
        )
        query_pos = (cycle_rank * per_shard + first + jnp.arange(group, dtype=jnp.int32))[
            :, None
        ] * BLOCK + within[None, :]
        key_pos = (listed_grp[:, :, None] * BLOCK + within[None, None, :]).reshape(
            group, extent * BLOCK
        )
        allowed = jnp.repeat(usable_grp, BLOCK, axis=1)[:, None, :] & (
            key_pos[:, None, :] <= query_pos[:, :, None]
        )
        row_max = jnp.max(jnp.where(allowed, scores, -1e30), axis=2)
        total = jnp.sum(jnp.where(allowed, jnp.exp(scores - row_max[:, :, None]), 0.0), axis=2)
        log_total = row_max + jnp.log(total)
        probs = jnp.where(allowed, jnp.exp(scores - log_total[:, :, None]), 0.0)
        prob_grad = jnp.einsum(
            "gqd,gkd->gqk", grad_grp, value_sel, preferred_element_type=jnp.float32
        )
        score_grad = (probs * (prob_grad - delta_grp[:, :, None]) * score_scale).astype(
            jnp.bfloat16
        )
        query_part = jnp.einsum(
            "gqk,gkd->gqd", score_grad, key_sel, preferred_element_type=jnp.float32
        ).astype(jnp.bfloat16)
        key_part = jnp.einsum(
            "gqk,gqd->gkd", score_grad, query_grp, preferred_element_type=jnp.float32
        )
        value_part = jnp.einsum(
            "gqk,gqd->gkd", probs.astype(jnp.bfloat16), grad_grp, preferred_element_type=jnp.float32
        )
        key_grad_store = key_grad_store.at[index_grp].add(
            key_part.reshape(group * extent, BLOCK, HD)
        )
        value_grad_store = value_grad_store.at[index_grp].add(
            value_part.reshape(group * extent, BLOCK, HD)
        )
        return ((key_grad_store, value_grad_store), query_part)

    zero_store = jnp.zeros((store_size, BLOCK, HD), jnp.float32)
    (key_grad_store, value_grad_store), query_parts = lax.scan(
        group_turn, (zero_store, zero_store), jnp.arange(group_count, dtype=jnp.int32)
    )
    query_acc = query_parts.reshape(shard_len, HD)
    key_acc = key_grad_store[:per_shard]
    value_acc = value_grad_store[:per_shard]
    far_key_grad = key_grad_store[per_shard + 2 :].reshape(cycle_size, CAP, BLOCK, HD)
    far_value_grad = value_grad_store[per_shard + 2 :].reshape(cycle_size, CAP, BLOCK, HD)
    dest_ids = jnp.arange(cycle_size, dtype=jnp.int32)
    to_prev = (dest_ids == cycle_rank - 1)[:, None, None]
    to_first = (dest_ids == 0)[:, None, None]
    extra_key_grad = jnp.stack(
        [
            jnp.where(to_prev, key_grad_store[per_shard][None], 0.0),
            jnp.where(to_first, key_grad_store[per_shard + 1][None], 0.0),
        ],
        axis=1,
    )
    extra_value_grad = jnp.stack(
        [
            jnp.where(to_prev, value_grad_store[per_shard][None], 0.0),
            jnp.where(to_first, value_grad_store[per_shard + 1][None], 0.0),
        ],
        axis=1,
    )
    all_key_back, all_value_back = (
        lax.all_to_all(
            jnp.concatenate([far_key_grad, extra_key_grad], axis=1),
            "blk",
            split_axis=0,
            concat_axis=0,
            tiled=True,
        ),
        lax.all_to_all(
            jnp.concatenate([far_value_grad, extra_value_grad], axis=1),
            "blk",
            split_axis=0,
            concat_axis=0,
            tiled=True,
        ),
    )
    back_key = all_key_back[:, :CAP]
    back_value = all_value_back[:, :CAP]
    prev_back = jnp.stack(
        [jnp.sum(all_key_back[:, CAP], axis=0), jnp.sum(all_value_back[:, CAP], axis=0)]
    )
    first_back = jnp.stack(
        [jnp.sum(all_key_back[:, CAP + 1], axis=0), jnp.sum(all_value_back[:, CAP + 1], axis=0)]
    )
    key_acc = key_acc.at[per_shard - 1].add(prev_back[0]).at[0].add(first_back[0])
    value_acc = value_acc.at[per_shard - 1].add(prev_back[1]).at[0].add(first_back[1])
    back_key = jnp.where(filled[:, :, None, None], back_key, 0.0).reshape(
        cycle_size * CAP, BLOCK, HD
    )
    back_value = jnp.where(filled[:, :, None, None], back_value, 0.0).reshape(
        cycle_size * CAP, BLOCK, HD
    )
    key_acc = key_acc.at[select.reshape(-1)].add(back_key).reshape(shard_len, HD)
    value_acc = value_acc.at[select.reshape(-1)].add(back_value).reshape(shard_len, HD)
    outgoing = (
        query_acc.reshape(shard_len, 1, HD),
        key_acc.astype(jnp.bfloat16).reshape(shard_len, 1, HD),
        value_acc.astype(jnp.bfloat16).reshape(shard_len, 1, HD),
    )
    query_back, key_back, value_back = (
        lax.all_to_all(outgoing[0], "uly", split_axis=0, concat_axis=1, tiled=True),
        lax.all_to_all(outgoing[1], "uly", split_axis=0, concat_axis=1, tiled=True),
        lax.all_to_all(outgoing[2], "uly", split_axis=0, concat_axis=1, tiled=True),
    )
    return (
        query_back.reshape(tok_count, head_count * HD),
        key_back.reshape(tok_count, head_count * HD),
        value_back.reshape(tok_count, head_count * HD),
    )


NEG = -1e30
KEY, QUERY, GRAD, VALUE = 0, 1, 2, 3
D_QUERY, D_KEY, D_VALUE = 0, 1, 2
ROWS_BY_COLS = (((1,), (1,)), ((), ()))
COLS_BY_COLS = (((0,), (0,)), ((), ()))


def flip(value, mask, count):
    if count & (count - 1):
        return lax.rem(value + mask, count)
    for bit in range(count.bit_length() - 1):
        if mask >> bit & 1:
            value = value + (1 << bit) * (1 - 2 * (value // (1 << bit) % 2))
    return value


def core_of(shard):
    return (shard + 1) // 2 % 2


def fused_kernel(
    shards,
    uly,
    picks_hbm,
    q_ref,
    k_ref,
    v_ref,
    o_ref,
    g_ref,
    out_ref,
    picks_ref,
    rows_in,
    held,
    delta_send,
    delta_recv,
    bias,
    stats,
    scores,
    probs_low,
    score_grads,
    acc,
    partial,
    outgoing,
    zs,
    zr,
    sb,
    st,
    pt,
    ds_sem,
    dr_sem,
    os_sem,
    or_sem,
    il,
):
    tok = q_ref.shape[0]
    length = tok * uly
    per = length // BLOCK
    gp = BLOCK // tok
    blocks = per * shards
    planes = uly // shards
    base = (uly // 2 - planes) // 2
    scale = HD ** (-0.5)
    f32 = jnp.float32
    b = lax.axis_index("blk")
    u = lax.axis_index("uly")
    uz, core = u // 2, u % 2
    plane = uz - base
    is_home = jnp.logical_and(plane >= 0, plane < planes)
    near = jnp.clip(plane, 0, planes - 1)
    head = b + shards * near
    own_source = jnp.logical_and(is_home, core_of(b) == core)
    inputs = {KEY: k_ref, QUERY: q_ref, VALUE: v_ref, GRAD: g_ref}
    mesh_ids = pl.DeviceIdType.MESH

    def home(h, s):
        return h % shards, (base + h // shards) * 2 + core_of(s)

    sibling = (b, uz * 2 + 1 - core)

    def is_self(place):
        return jnp.logical_and(place[0] == b, place[1] == u)

    def ids(place):
        return {"blk": place[0], "uly": place[1]}

    def cols(p):
        return pl.ds(pl.multiple_of(p * HD, HD), HD)

    def rows(p):
        return pl.ds(pl.multiple_of(p * tok, tok), tok)

    def remote(source, target, send, recv, place):
        return pltpu.make_async_remote_copy(
            src_ref=source,
            dst_ref=target,
            send_sem=send,
            recv_sem=recv,
            device_id=ids(place),
            device_id_type=mesh_ids,
        )

    def ship(source, target, send, recv, place, maybe_here):
        if not maybe_here:
            remote(source, target, send, recv, place).start()
            return
        mine = is_self(place)

        @pl.when(jnp.logical_not(mine))
        def _():
            remote(source, target, send, recv, place).start()

        @pl.when(mine)
        def _():
            pltpu.make_async_copy(source, target, recv).start()

    def heads():
        return [(flip(head, mask, uly), mask == 0) for mask in reversed(range(uly))]

    def z_send(t):
        for h, maybe_here in heads():
            ship(
                inputs[t].at[:, cols(h)],
                held.at[t, b, rows(u), :],
                zs.at[0],
                zr.at[t, b // 2],
                home(h, b),
                maybe_here,
            )

    fetches = (
        pltpu.make_async_copy(o_ref, rows_in.at[0], il.at[0]),
        pltpu.make_async_copy(g_ref, rows_in.at[1], il.at[1]),
        pltpu.make_async_copy(picks_hbm, picks_ref, il.at[2]),
    )
    barrier = pltpu.get_barrier_semaphore()

    def greet(place):
        pl.semaphore_signal(barrier, inc=1, device_id=ids(place), device_id_type=mesh_ids)

    with jax.named_scope("greet"):

        @pl.when(is_home)
        def _():
            for j in range(shards // 2):
                s = 2 * j + (core + j) % 2
                for mask in reversed(range(uly)):
                    place = (s, flip(u, mask, uly))
                    pl.when(jnp.logical_not(is_self(place)))(functools.partial(greet, place))
            greet(sibling)

        for fetch in fetches:
            fetch.start()
    with jax.named_scope("barrier"):
        pl.semaphore_wait(
            barrier, uly - jnp.where(own_source, 1, 0) + jnp.where(is_home, 1, 0)
        )
    with jax.named_scope("send_kq"):
        z_send(KEY)
        z_send(QUERY)

    with jax.named_scope("prep"):
        for fetch in fetches:
            fetch.wait()
        product = rows_in[0].astype(f32) * rows_in[1].astype(f32)
        high = product.astype(jnp.bfloat16)
        low = (product - high.astype(f32)).astype(jnp.bfloat16)
        head_of = lax.broadcasted_iota(jnp.int32, (uly, uly * HD), 1) // HD
        pick_head = jnp.where(
            head_of == lax.broadcasted_iota(jnp.int32, (uly, uly * HD), 0), 1.0, 0.0
        ).astype(jnp.bfloat16)
        sums = sum(
            lax.dot_general(
                pick_head,
                jnp.concatenate([part] * gp, axis=0),
                ROWS_BY_COLS,
                preferred_element_type=f32,
            )
            for part in (high, low)
        )
        place_of = lax.broadcasted_iota(jnp.int32, (uly, BLOCK), 1) // tok
        sums = jnp.where(place_of == lax.rem(u, gp), sums, 0.0)
        for h in range(uly):
            delta_send[h] = sums[h : h + 1]

    with jax.named_scope("send_gv"):
        for h, maybe_here in heads():
            ship(
                delta_send.at[h],
                delta_recv.at[b // 2, u],
                ds_sem.at[0],
                dr_sem.at[0],
                home(h, b),
                maybe_here,
            )
        z_send(GRAD)
        z_send(VALUE)

    def at(jb):
        return pl.ds(jb * BLOCK, BLOCK)

    def run_home(c):
        owned = [s for s in range(shards) if core_of(s) == c]
        foreign = [s for s in range(shards) if core_of(s) != c and s > owned[0]]
        lent = [s for s in owned if any(core_of(k) != c and k < s for k in range(shards))]
        tiles = [(q, k) for k in owned for q in range(k, shards)]
        slot = {tile: n for n, tile in enumerate(tiles)}
        q_all = sorted({q for q, _ in tiles})
        q_own = [q for q in q_all if q in owned]
        q_far = [q for q in q_all if q not in owned]
        pair_of = {QUERY: 0, GRAD: 1}

        def own(t):
            with jax.named_scope(f"own_{t}"):
                for s in owned:
                    ref = held.at[t, s]
                    remote(ref, ref, zs.at[0], zr.at[t, s // 2], (b, u)).wait_recv()
                    if t in pair_of and s in lent:
                        sem = sb.at[pair_of[t], s]
                        remote(ref, ref, sem, sem, sibling).start()

        def lent_copy(t, s):
            sem = sb.at[pair_of[t], s]
            return remote(held.at[t, s], held.at[t, s], sem, sem, sibling)

        def tile_first(q, k, jb):
            return jb * BLOCK if q == k else 0

        def widen(row, first, fill):
            if first:
                return jnp.concatenate([jnp.full((1, first), fill, f32), row], axis=1)
            return row

        def make_scores(q, k, top):
            with jax.named_scope(f"scores_{q}_{k}"):
                for jb in range(per):
                    first = tile_first(q, k, jb)
                    tile = lax.dot_general(
                        held[KEY, k, at(jb), :],
                        held[QUERY, q, first:, :],
                        ROWS_BY_COLS,
                        preferred_element_type=f32,
                    )
                    tile = tile * scale + bias[q, pl.ds(k * per + jb, 1), first:]
                    if q == k:
                        wide = length - first
                        key_at = lax.broadcasted_iota(jnp.int32, (BLOCK, wide), 0)
                        query_at = lax.broadcasted_iota(jnp.int32, (BLOCK, wide), 1)
                        tile = jnp.where(key_at <= query_at, tile, NEG)
                    scores[slot[q, k], at(jb), first:] = tile
                    high = widen(jnp.max(tile, axis=0, keepdims=True), first, NEG)
                    top = high if top is None else jnp.maximum(top, high)
            return top

        def make_exps(q, top):
            with jax.named_scope(f"exps_{q}"):
                total = jnp.zeros((1, length), f32)
                for k in owned:
                    if k > q:
                        continue
                    for jb in range(per):
                        first = tile_first(q, k, jb)
                        tile = jnp.exp(scores[slot[q, k], at(jb), first:] - top[:, first:])
                        scores[slot[q, k], at(jb), first:] = tile
                        part = jnp.sum(tile, axis=0, keepdims=True)
                        total = total + widen(part, first, 0.0)
                stats[c, q, 0:1, :] = top
                stats[c, q, 1:2, :] = total

        def make_probs(q, k, factor):
            with jax.named_scope(f"probs_{q}_{k}"):
                for jb in range(per):
                    first = tile_first(q, k, jb)
                    probs = scores[slot[q, k], at(jb), first:] * factor[:, first:]
                    if first:
                        blank = jnp.zeros((BLOCK, first), jnp.bfloat16)
                        probs_low[slot[q, k], at(jb), :first] = blank
                    probs_low[slot[q, k], at(jb), first:] = probs.astype(jnp.bfloat16)

        def add(ref, value, fresh):
            if fresh:
                ref[...] = value
            else:
                ref[...] += value

        def make_values(q, k, fresh):
            with jax.named_scope(f"values_{q}_{k}"):
                product = jnp.dot(
                    probs_low[slot[q, k]], held[GRAD, q], preferred_element_type=f32
                )
                add(acc.at[D_VALUE, k], product, fresh)

        def make_grads(q, k, factor, delta):
            with jax.named_scope(f"grads_{q}_{k}"):
                for jb in range(per):
                    first = tile_first(q, k, jb)
                    prob_grad = lax.dot_general(
                        held[VALUE, k, at(jb), :],
                        held[GRAD, q, first:, :],
                        ROWS_BY_COLS,
                        preferred_element_type=f32,
                    )
                    grads = (scores[slot[q, k], at(jb), first:] * factor[:, first:]) * (
                        prob_grad - delta[:, first:]
                    )
                    if first:
                        score_grads[at(jb), :first] = jnp.zeros((BLOCK, first), jnp.bfloat16)
                    score_grads[at(jb), first:] = grads.astype(jnp.bfloat16)

        def add_query(q, k, fresh):
            product = lax.dot_general(
                score_grads[...], held[KEY, k], COLS_BY_COLS, preferred_element_type=f32
            )
            add(acc.at[D_QUERY, q], product, fresh)

        def add_key(q, k, fresh):
            product = jnp.dot(score_grads[...], held[QUERY, q], preferred_element_type=f32)
            add(acc.at[D_KEY, k], product, fresh)

        def send_result(t, s):
            with jax.named_scope(f"send_{t}_{s}"):
                outgoing[t, s // 2] = acc[t, s].astype(jnp.bfloat16)
                for mask in list(range(1, uly)) + [0]:
                    p = flip(u, mask, uly)
                    ship(
                        outgoing.at[t, s // 2, rows(p), :],
                        out_ref.at[t, :, cols(head)],
                        os_sem.at[0],
                        or_sem.at[0],
                        (s, p),
                        mask == 0,
                    )

        own(KEY)
        own(QUERY)
        tops = {}
        for q in q_own:
            for k in owned:
                if k <= q:
                    tops[q] = make_scores(q, k, tops.get(q))
        for q in q_own:
            make_exps(q, tops[q])
        for q in q_far:
            with jax.named_scope("lent_q"):
                lent_copy(QUERY, q).wait_recv()
            for k in owned:
                if k <= q:
                    tops[q] = make_scores(q, k, tops.get(q))
            make_exps(q, tops[q])
        with jax.named_scope("stats"):
            remote(delta_recv, delta_recv, ds_sem.at[0], dr_sem.at[0], (b, u)).wait_recv()
            for s in owned:
                pieces = []
                for n in range(per):
                    piece = delta_recv[s // 2, n * gp]
                    for i in range(1, gp):
                        piece = piece + delta_recv[s // 2, n * gp + i]
                    pieces.append(piece)
                stats[c, s, 2:3, :] = jnp.concatenate(pieces, axis=1)
            remote(stats.at[c], stats.at[c], st.at[c], st.at[c], sibling).start()
        own(GRAD)
        with jax.named_scope("stats_wait"):
            remote(stats.at[1 - c], stats.at[1 - c], st.at[c], st.at[1 - c], sibling).wait_recv()
        factors, deltas = {}, {}
        for q in q_all:
            top, total = stats[c, q, 0:1, :], stats[c, q, 1:2, :]
            if any(core_of(k) != c for k in range(q + 1)):
                top_far, total_far = stats[1 - c, q, 0:1, :], stats[1 - c, q, 1:2, :]
                high = jnp.maximum(top, top_far)
                share = jnp.exp(top - high)
                factors[q] = share / (share * total + jnp.exp(top_far - high) * total_far)
            else:
                factors[q] = 1.0 / total
            deltas[q] = stats[c if q in owned else 1 - c, q, 2:3, :]
        started = set()

        def starts(*what):
            new = what not in started
            started.add(what)
            return new

        have = set(q_own)
        for k in reversed(owned):
            for q in q_own + q_far:
                if k > q:
                    continue
                make_probs(q, k, factors[q])
                if q not in have:
                    with jax.named_scope("lent_g"):
                        lent_copy(GRAD, q).wait_recv()
                    have.add(q)
                make_values(q, k, starts("v", k))
            send_result(D_VALUE, k)
        own(VALUE)
        for k in reversed(owned):
            for q in q_far + q_own:
                if k > q:
                    continue
                make_grads(q, k, factors[q] * scale, deltas[q])
                with jax.named_scope(f"dots_{q}_{k}"):
                    add_query(q, k, starts("q", q))
                    add_key(q, k, starts("k", k))
                if k == owned[0] and q in q_far:
                    ref = acc.at[D_QUERY, q]
                    remote(ref, partial.at[q], pt.at[q], pt.at[q], sibling).start()
            send_result(D_KEY, k)
        for q in q_own:
            if q in lent:
                with jax.named_scope("partial"):
                    ref = partial.at[q]
                    remote(ref, ref, pt.at[q], pt.at[q], sibling).wait_recv()
                    acc[D_QUERY, q] += partial[q]
            send_result(D_QUERY, q)
        with jax.named_scope("lent_sent"):
            for s in lent:
                for t in pair_of:
                    lent_copy(t, s).wait_send()
            for q in q_far:
                ref = acc.at[D_QUERY, q]
                remote(ref, ref, pt.at[q], pt.at[q], sibling).wait_send()
            remote(stats.at[c], stats.at[c], st.at[c], st.at[c], sibling).wait_send()

    @pl.when(is_home)
    def _():
        with jax.named_scope("bias"):
            lane_block = lax.broadcasted_iota(jnp.int32, (1, length), 1) // BLOCK
            key_block = lax.broadcasted_iota(jnp.int32, (blocks, length), 0)
            for s in range(shards):
                query_block = lane_block + s * per
                hit = (key_block == query_block) | (key_block == query_block - 1)
                hit = hit | (key_block == 0)
                for r in range(RAND):
                    named = jnp.zeros((1, length), jnp.int32)
                    for i in range(per):
                        named = jnp.where(lane_block == i, picks_ref[r, s * per + i], named)
                    hit = hit | (key_block == named)
                hit = hit & (key_block <= query_block)
                bias[s] = jnp.where(hit, 0.0, NEG)
        for c in range(2):
            pl.when(core == c)(functools.partial(run_home, c))

    def drain(count):
        ref = held.at[:, 0, pl.ds(0, count * tok), :]
        remote(ref, ref, zs.at[0], zr.at[0, 0], (b, u)).wait_send()
        ref = delta_send.at[pl.ds(0, count)]
        remote(ref, ref, ds_sem.at[0], dr_sem.at[0], (b, u)).wait_send()

    with jax.named_scope("sent"):
        pl.when(own_source)(lambda: drain(uly - 1))
        pl.when(jnp.logical_not(own_source))(lambda: drain(uly))

        @pl.when(own_source)
        def _():
            ref = outgoing.at[:, :, pl.ds(0, length - tok // (shards // 2)), :]
            remote(ref, ref, os_sem.at[0], or_sem.at[0], (b, u)).wait_send()

        @pl.when(jnp.logical_and(is_home, jnp.logical_not(own_source)))
        def _():
            remote(outgoing, outgoing, os_sem.at[0], or_sem.at[0], (b, u)).wait_send()

    with jax.named_scope("landed"):
        remote(out_ref, out_ref, os_sem.at[0], or_sem.at[0], (b, u)).wait_recv()


def write_out(held, a_out, b_out, c_out, done):
    writes = [
        pltpu.make_async_copy(held.at[i], target, done.at[i])
        for i, target in enumerate((a_out, b_out, c_out))
    ]
    for write in writes:
        write.start()
    for write in writes:
        write.wait()


def fused_on_device(shards, uly, q, k, v, o, g, random_blocks):
    tok, width = q.shape
    length = tok * uly
    per = length // BLOCK
    half = shards // 2
    tiles = max(
        sum(shards - k for k in range(shards) if core_of(k) == core) for core in range(2)
    )
    dma = pltpu.SemaphoreType.DMA
    hbm = pl.BlockSpec(memory_space=pltpu.HBM)
    vmem = pl.BlockSpec(memory_space=pltpu.VMEM)
    placed = [
        pltpu.with_memory_space_constraint(x, pltpu.HBM) for x in (random_blocks.T, q, k, v, o, g)
    ]
    results = pl.pallas_call(
        functools.partial(fused_kernel, shards, uly),
        out_shape=jax.ShapeDtypeStruct((3, tok, width), jnp.bfloat16),
        in_specs=[hbm] * 6,
        out_specs=vmem,
        scratch_shapes=[
            pltpu.SMEM(random_blocks.shape[::-1], jnp.int32),
            pltpu.VMEM((2, tok, width), jnp.bfloat16),
            pltpu.VMEM((4, shards, length, HD), jnp.bfloat16),
            pltpu.VMEM((uly, 1, BLOCK), jnp.float32),
            pltpu.VMEM((half, uly, 1, BLOCK), jnp.float32),
            pltpu.VMEM((shards, shards * per, length), jnp.float32),
            pltpu.VMEM((2, shards, 3, length), jnp.float32),
            pltpu.VMEM((tiles, length, length), jnp.float32),
            pltpu.VMEM((tiles, length, length), jnp.bfloat16),
            pltpu.VMEM((length, length), jnp.bfloat16),
            pltpu.VMEM((3, shards, length, HD), jnp.float32),
            pltpu.VMEM((shards, length, HD), jnp.float32),
            pltpu.VMEM((3, half, length, HD), jnp.bfloat16),
            dma((1,)),
            dma((4, half)),
            dma((2, shards)),
            dma((2,)),
            dma((shards,)),
            dma((1,)),
            dma((1,)),
            dma((1,)),
            dma((1,)),
            dma((3,)),
        ],
        compiler_params=pltpu.CompilerParams(
            collective_id=0, has_side_effects=True, vmem_limit_bytes=32 * 1024 * 1024
        ),
    )(*placed)
    return pl.pallas_call(
        write_out,
        out_shape=[jax.ShapeDtypeStruct((tok, width), jnp.bfloat16)] * 3,
        in_specs=[vmem],
        out_specs=[hbm] * 3,
        scratch_shapes=[dma((3,))],
        compiler_params=pltpu.CompilerParams(vmem_limit_bytes=32 * 1024 * 1024),
    )(results)


def wide_or_fused(shards, uly, *operands):
    tok, width = operands[0].shape
    length = tok * uly
    fits = shards * length * length * 4 <= 4 * 1024 * 1024
    paired = shards % 4 == 0 and uly % shards == 0
    if fits and paired and width == uly * HD and BLOCK % tok == 0 and length % BLOCK == 0:
        return tuple(fused_on_device(shards, uly, *operands))
    return on_device(*operands)


def solution(mesh):
    return jax.shard_map(
        functools.partial(wide_or_fused, mesh.shape["blk"], mesh.shape["uly"]),
        mesh=mesh,
        in_specs=(
            P(("blk", "uly"), None),
            P(("blk", "uly"), None),
            P(("blk", "uly"), None),
            P(("blk", "uly"), None),
            P(("blk", "uly"), None),
            P(),
        ),
        out_specs=(P(("blk", "uly"), None), P(("blk", "uly"), None), P(("blk", "uly"), None)),
        check_vma=False,
    )
```

```python
import functools
import math

import jax
import jax.numpy as jnp
from jax import lax
from jax.experimental import pallas as pl
from jax.experimental.pallas import tpu as pltpu
from jax.sharding import PartitionSpec as P

HD = 128
BLOCK = 128
RAND = 3
CAP = 2


def named_table(random_blocks, per_shard):
    block_count = random_blocks.shape[0]
    shard_count = block_count // per_shard
    entries = random_blocks.reshape(shard_count, per_shard * RAND)
    block_ids = jnp.arange(block_count, dtype=jnp.int32)
    named = jnp.any(entries[:, :, None] == block_ids[None, None, :], axis=1)
    owner = block_ids // per_shard
    named = named & (owner[None, :] != jnp.arange(shard_count, dtype=jnp.int32)[:, None])
    grouped = named.reshape(shard_count, shard_count, per_shard).astype(jnp.int32)
    rank_in = jnp.cumsum(grouped, axis=2) - grouped
    return (grouped, rank_in)


def send_slots(grouped, rank_in, cycle_rank, per_shard):
    mine = lax.dynamic_index_in_dim(grouped, cycle_rank, 1, keepdims=False)
    mine_rank = lax.dynamic_index_in_dim(rank_in, cycle_rank, 1, keepdims=False)
    slot_ids = jnp.arange(CAP, dtype=jnp.int32)
    hit = (mine[:, None, :] == 1) & (mine_rank[:, None, :] == slot_ids[None, :, None])
    positions = jnp.arange(per_shard, dtype=jnp.int32)
    select = jnp.sum(jnp.where(hit, positions[None, None, :], 0), axis=2)
    filled = jnp.any(hit, axis=2)
    return (select, filled)


def on_device(query_proj, key_proj, value_proj, attn_output, out_grad, random_blocks):
    tok_count = query_proj.shape[0]
    head_count = query_proj.shape[1] // HD
    score_scale = HD ** (-0.5)
    extent = 3 + RAND

    def to_heads(tensor):
        return tensor.reshape(tok_count, head_count, HD)

    query_rows, key_rows, value_rows, output_rows, grad_rows = (
        lax.all_to_all(to_heads(query_proj), "uly", split_axis=1, concat_axis=0, tiled=True),
        lax.all_to_all(to_heads(key_proj), "uly", split_axis=1, concat_axis=0, tiled=True),
        lax.all_to_all(to_heads(value_proj), "uly", split_axis=1, concat_axis=0, tiled=True),
        lax.all_to_all(to_heads(attn_output), "uly", split_axis=1, concat_axis=0, tiled=True),
        lax.all_to_all(to_heads(out_grad), "uly", split_axis=1, concat_axis=0, tiled=True),
    )
    row_delta = jnp.sum(
        output_rows.astype(jnp.float32) * grad_rows.astype(jnp.float32), axis=2
    ).reshape(-1)
    shard_len = query_rows.shape[0]
    per_shard = shard_len // BLOCK
    query_blocks = query_rows.reshape(per_shard, BLOCK, HD)
    key_blocks = key_rows.reshape(per_shard, BLOCK, HD)
    value_blocks = value_rows.reshape(per_shard, BLOCK, HD)
    grad_blocks = grad_rows.reshape(per_shard, BLOCK, HD)
    delta_blocks = row_delta.reshape(per_shard, BLOCK)
    cycle_size = lax.axis_size("blk")
    cycle_rank = lax.axis_index("blk")
    block_count = random_blocks.shape[0]
    grouped, rank_in = named_table(random_blocks, per_shard)
    select, filled = send_slots(grouped, rank_in, cycle_rank, per_shard)
    key_send = jnp.where(
        filled[:, :, None, None],
        jnp.take(key_blocks, select.reshape(-1), axis=0).reshape(cycle_size, CAP, BLOCK, HD),
        jnp.zeros((), jnp.bfloat16),
    )
    value_send = jnp.where(
        filled[:, :, None, None],
        jnp.take(value_blocks, select.reshape(-1), axis=0).reshape(cycle_size, CAP, BLOCK, HD),
        jnp.zeros((), jnp.bfloat16),
    )
    extra_key = jnp.broadcast_to(
        jnp.stack([key_blocks[per_shard - 1], key_blocks[0]])[None], (cycle_size, 2, BLOCK, HD)
    )
    extra_value = jnp.broadcast_to(
        jnp.stack([value_blocks[per_shard - 1], value_blocks[0]])[None], (cycle_size, 2, BLOCK, HD)
    )
    all_key, all_value = (
        lax.all_to_all(
            jnp.concatenate([key_send, extra_key], axis=1),
            "blk",
            split_axis=0,
            concat_axis=0,
            tiled=True,
        ),
        lax.all_to_all(
            jnp.concatenate([value_send, extra_value], axis=1),
            "blk",
            split_axis=0,
            concat_axis=0,
            tiled=True,
        ),
    )
    far_key = all_key[:, :CAP]
    far_value = all_value[:, :CAP]
    before_rank = jnp.maximum(cycle_rank - 1, 0)
    prev_key = lax.dynamic_index_in_dim(all_key, before_rank, 0, keepdims=False)[CAP]
    prev_value = lax.dynamic_index_in_dim(all_value, before_rank, 0, keepdims=False)[CAP]
    first_key = all_key[0, CAP + 1]
    first_value = all_value[0, CAP + 1]
    key_store = jnp.concatenate(
        [key_blocks, prev_key[None], first_key[None], far_key.reshape(cycle_size * CAP, BLOCK, HD)],
        axis=0,
    )
    value_store = jnp.concatenate(
        [
            value_blocks,
            prev_value[None],
            first_value[None],
            far_value.reshape(cycle_size * CAP, BLOCK, HD),
        ],
        axis=0,
    )
    store_size = key_store.shape[0]
    picked = lax.dynamic_slice_in_dim(random_blocks, cycle_rank * per_shard, per_shard, 0)
    own_rank = lax.dynamic_index_in_dim(rank_in, cycle_rank, 0, keepdims=False).reshape(-1)
    all_ids = jnp.arange(block_count, dtype=jnp.int32)
    slot_of = jnp.sum(
        jnp.where(picked[:, :, None] == all_ids[None, None, :], own_rank[None, None, :], 0), axis=2
    )
    owner = picked // per_shard
    random_index = jnp.where(
        owner == cycle_rank, picked - cycle_rank * per_shard, per_shard + 2 + owner * CAP + slot_of
    )
    local_ids = jnp.arange(per_shard, dtype=jnp.int32)
    global_ids = cycle_rank * per_shard + local_ids
    listed = jnp.concatenate(
        [
            global_ids[:, None],
            global_ids[:, None] - 1,
            jnp.zeros((per_shard, 1), jnp.int32),
            picked,
        ],
        axis=1,
    )
    first_index = jnp.zeros((per_shard, 1), jnp.int32) + jnp.where(
        cycle_rank == 0, 0, per_shard + 1
    ).astype(jnp.int32)
    store_index = jnp.concatenate(
        [
            local_ids[:, None],
            jnp.where(local_ids >= 1, local_ids - 1, per_shard)[:, None],
            first_index,
            random_index,
        ],
        axis=1,
    )
    order = jnp.arange(extent, dtype=jnp.int32)
    earlier = order[None, :] < order[:, None]
    repeated = jnp.any((listed[:, :, None] == listed[:, None, :]) & earlier[None, :, :], axis=2)
    usable = (listed >= 0) & jnp.logical_not(repeated)
    within = jnp.arange(BLOCK, dtype=jnp.int32)
    group = math.gcd(per_shard, max(1, 512 // BLOCK))
    group_count = per_shard // group

    def group_turn(carry, group_index):
        key_grad_store, value_grad_store = carry
        first = group_index * group
        query_grp = lax.dynamic_slice_in_dim(query_blocks, first, group, 0)
        grad_grp = lax.dynamic_slice_in_dim(grad_blocks, first, group, 0)
        delta_grp = lax.dynamic_slice_in_dim(delta_blocks, first, group, 0)
        index_grp = lax.dynamic_slice_in_dim(store_index, first, group, 0).reshape(-1)
        listed_grp = lax.dynamic_slice_in_dim(listed, first, group, 0)
        usable_grp = lax.dynamic_slice_in_dim(usable, first, group, 0)
        key_sel = jnp.take(key_store, index_grp, axis=0).reshape(group, extent * BLOCK, HD)
        value_sel = jnp.take(value_store, index_grp, axis=0).reshape(group, extent * BLOCK, HD)
        scores = (
            jnp.einsum("gqd,gkd->gqk", query_grp, key_sel, preferred_element_type=jnp.float32)
            * score_scale
        )
        query_pos = (cycle_rank * per_shard + first + jnp.arange(group, dtype=jnp.int32))[
            :, None
        ] * BLOCK + within[None, :]
        key_pos = (listed_grp[:, :, None] * BLOCK + within[None, None, :]).reshape(
            group, extent * BLOCK
        )
        allowed = jnp.repeat(usable_grp, BLOCK, axis=1)[:, None, :] & (
            key_pos[:, None, :] <= query_pos[:, :, None]
        )
        row_max = jnp.max(jnp.where(allowed, scores, -1e30), axis=2)
        total = jnp.sum(jnp.where(allowed, jnp.exp(scores - row_max[:, :, None]), 0.0), axis=2)
        log_total = row_max + jnp.log(total)
        probs = jnp.where(allowed, jnp.exp(scores - log_total[:, :, None]), 0.0)
        prob_grad = jnp.einsum(
            "gqd,gkd->gqk", grad_grp, value_sel, preferred_element_type=jnp.float32
        )
        score_grad = (probs * (prob_grad - delta_grp[:, :, None]) * score_scale).astype(
            jnp.bfloat16
        )
        query_part = jnp.einsum(
            "gqk,gkd->gqd", score_grad, key_sel, preferred_element_type=jnp.float32
        ).astype(jnp.bfloat16)
        key_part = jnp.einsum(
            "gqk,gqd->gkd", score_grad, query_grp, preferred_element_type=jnp.float32
        )
        value_part = jnp.einsum(
            "gqk,gqd->gkd", probs.astype(jnp.bfloat16), grad_grp, preferred_element_type=jnp.float32
        )
        key_grad_store = key_grad_store.at[index_grp].add(
            key_part.reshape(group * extent, BLOCK, HD)
        )
        value_grad_store = value_grad_store.at[index_grp].add(
            value_part.reshape(group * extent, BLOCK, HD)
        )
        return ((key_grad_store, value_grad_store), query_part)

    zero_store = jnp.zeros((store_size, BLOCK, HD), jnp.float32)
    (key_grad_store, value_grad_store), query_parts = lax.scan(
        group_turn, (zero_store, zero_store), jnp.arange(group_count, dtype=jnp.int32)
    )
    query_acc = query_parts.reshape(shard_len, HD)
    key_acc = key_grad_store[:per_shard]
    value_acc = value_grad_store[:per_shard]
    far_key_grad = key_grad_store[per_shard + 2 :].reshape(cycle_size, CAP, BLOCK, HD)
    far_value_grad = value_grad_store[per_shard + 2 :].reshape(cycle_size, CAP, BLOCK, HD)
    dest_ids = jnp.arange(cycle_size, dtype=jnp.int32)
    to_prev = (dest_ids == cycle_rank - 1)[:, None, None]
    to_first = (dest_ids == 0)[:, None, None]
    extra_key_grad = jnp.stack(
        [
            jnp.where(to_prev, key_grad_store[per_shard][None], 0.0),
            jnp.where(to_first, key_grad_store[per_shard + 1][None], 0.0),
        ],
        axis=1,
    )
    extra_value_grad = jnp.stack(
        [
            jnp.where(to_prev, value_grad_store[per_shard][None], 0.0),
            jnp.where(to_first, value_grad_store[per_shard + 1][None], 0.0),
        ],
        axis=1,
    )
    all_key_back, all_value_back = (
        lax.all_to_all(
            jnp.concatenate([far_key_grad, extra_key_grad], axis=1),
            "blk",
            split_axis=0,
            concat_axis=0,
            tiled=True,
        ),
        lax.all_to_all(
            jnp.concatenate([far_value_grad, extra_value_grad], axis=1),
            "blk",
            split_axis=0,
            concat_axis=0,
            tiled=True,
        ),
    )
    back_key = all_key_back[:, :CAP]
    back_value = all_value_back[:, :CAP]
    prev_back = jnp.stack(
        [jnp.sum(all_key_back[:, CAP], axis=0), jnp.sum(all_value_back[:, CAP], axis=0)]
    )
    first_back = jnp.stack(
        [jnp.sum(all_key_back[:, CAP + 1], axis=0), jnp.sum(all_value_back[:, CAP + 1], axis=0)]
    )
    key_acc = key_acc.at[per_shard - 1].add(prev_back[0]).at[0].add(first_back[0])
    value_acc = value_acc.at[per_shard - 1].add(prev_back[1]).at[0].add(first_back[1])
    back_key = jnp.where(filled[:, :, None, None], back_key, 0.0).reshape(
        cycle_size * CAP, BLOCK, HD
    )
    back_value = jnp.where(filled[:, :, None, None], back_value, 0.0).reshape(
        cycle_size * CAP, BLOCK, HD
    )
    key_acc = key_acc.at[select.reshape(-1)].add(back_key).reshape(shard_len, HD)
    value_acc = value_acc.at[select.reshape(-1)].add(back_value).reshape(shard_len, HD)
    outgoing = (
        query_acc.reshape(shard_len, 1, HD),
        key_acc.astype(jnp.bfloat16).reshape(shard_len, 1, HD),
        value_acc.astype(jnp.bfloat16).reshape(shard_len, 1, HD),
    )
    query_back, key_back, value_back = (
        lax.all_to_all(outgoing[0], "uly", split_axis=0, concat_axis=1, tiled=True),
        lax.all_to_all(outgoing[1], "uly", split_axis=0, concat_axis=1, tiled=True),
        lax.all_to_all(outgoing[2], "uly", split_axis=0, concat_axis=1, tiled=True),
    )
    return (
        query_back.reshape(tok_count, head_count * HD),
        key_back.reshape(tok_count, head_count * HD),
        value_back.reshape(tok_count, head_count * HD),
    )


NEG = -1e30
KEY, QUERY, GRAD, VALUE = 0, 1, 2, 3
D_QUERY, D_KEY, D_VALUE = 0, 1, 2
ROWS_BY_COLS = (((1,), (1,)), ((), ()))
COLS_BY_COLS = (((0,), (0,)), ((), ()))


FIRST_TILES = ((0, 0), (1, 0), (2, 0), (3, 0), (3, 3), (3, 2), (2, 2), (1, 1), (3, 1), (2, 1))


def flip(value, mask, count):
    if count & (count - 1):
        return lax.rem(value + mask, count)
    for bit in range(count.bit_length() - 1):
        if mask >> bit & 1:
            value = value + (1 << bit) * (1 - 2 * (value // (1 << bit) % 2))
    return value


def core_of(shard):
    return (shard + 1) // 2 % 2


def fused_kernel(
    shards,
    uly,
    picks_hbm,
    q_ref,
    k_ref,
    v_ref,
    o_ref,
    g_ref,
    out_ref,
    picks_ref,
    rows_in,
    held,
    delta_send,
    delta_recv,
    bias,
    stats,
    scores,
    probs_low,
    score_grads,
    acc,
    partial,
    outgoing,
    zs,
    zr,
    sb,
    st,
    pt,
    ds_sem,
    dr_sem,
    os_sem,
    or_sem,
    il,
):
    tok = q_ref.shape[0]
    length = tok * uly
    per = length // BLOCK
    gp = BLOCK // tok
    blocks = per * shards
    planes = uly // shards
    base = (uly // 2 - planes) // 2
    scale = HD ** (-0.5)
    f32 = jnp.float32
    b = lax.axis_index("blk")
    u = lax.axis_index("uly")
    uz, core = u // 2, u % 2
    plane = uz - base
    is_home = jnp.logical_and(plane >= 0, plane < planes)
    near = jnp.clip(plane, 0, planes - 1)
    head = b + shards * near
    own_source = jnp.logical_and(is_home, core_of(b) == core)
    inputs = {KEY: k_ref, QUERY: q_ref, VALUE: v_ref, GRAD: g_ref}
    mesh_ids = pl.DeviceIdType.MESH

    def home(h, s):
        return h % shards, (base + h // shards) * 2 + core_of(s)

    sibling = (b, uz * 2 + 1 - core)

    def is_self(place):
        return jnp.logical_and(place[0] == b, place[1] == u)

    def ids(place):
        return {"blk": place[0], "uly": place[1]}

    def cols(p):
        return pl.ds(pl.multiple_of(p * HD, HD), HD)

    def rows(p):
        return pl.ds(pl.multiple_of(p * tok, tok), tok)

    def remote(source, target, send, recv, place):
        return pltpu.make_async_remote_copy(
            src_ref=source,
            dst_ref=target,
            send_sem=send,
            recv_sem=recv,
            device_id=ids(place),
            device_id_type=mesh_ids,
        )

    def ship(source, target, send, recv, place, maybe_here):
        if not maybe_here:
            remote(source, target, send, recv, place).start()
            return
        mine = is_self(place)

        @pl.when(jnp.logical_not(mine))
        def _():
            remote(source, target, send, recv, place).start()

        @pl.when(mine)
        def _():
            pltpu.make_async_copy(source, target, recv).start()

    def heads():
        return [(flip(head, mask, uly), mask == 0) for mask in reversed(range(uly))]

    def z_send(t):
        for h, maybe_here in heads():
            ship(
                inputs[t].at[:, cols(h)],
                held.at[t, b, rows(u), :],
                zs.at[0],
                zr.at[t, b // 2, u // (uly // 2)],
                home(h, b),
                maybe_here,
            )

    fetches = (
        pltpu.make_async_copy(o_ref, rows_in.at[0], il.at[0]),
        pltpu.make_async_copy(g_ref, rows_in.at[1], il.at[1]),
        pltpu.make_async_copy(picks_hbm, picks_ref, il.at[2]),
    )
    barrier = pltpu.get_barrier_semaphore()

    def greet(place):
        pl.semaphore_signal(barrier, inc=1, device_id=ids(place), device_id_type=mesh_ids)

    with jax.named_scope("greet"):

        @pl.when(is_home)
        def _():
            for j in range(shards // 2):
                s = 2 * j + (core + j) % 2
                for mask in reversed(range(uly)):
                    place = (s, flip(u, mask, uly))
                    pl.when(jnp.logical_not(is_self(place)))(functools.partial(greet, place))
            greet(sibling)

        for fetch in fetches:
            fetch.start()
    with jax.named_scope("barrier"):
        pl.semaphore_wait(
            barrier, uly - jnp.where(own_source, 1, 0) + jnp.where(is_home, 1, 0)
        )
    with jax.named_scope("send_kq"):
        z_send(KEY)
        z_send(QUERY)

    with jax.named_scope("prep"):
        for fetch in fetches:
            fetch.wait()
        product = rows_in[0].astype(f32) * rows_in[1].astype(f32)
        high = product.astype(jnp.bfloat16)
        low = (product - high.astype(f32)).astype(jnp.bfloat16)
        head_of = lax.broadcasted_iota(jnp.int32, (uly, uly * HD), 1) // HD
        pick_head = jnp.where(
            head_of == lax.broadcasted_iota(jnp.int32, (uly, uly * HD), 0), 1.0, 0.0
        ).astype(jnp.bfloat16)
        sums = sum(
            lax.dot_general(
                pick_head,
                jnp.concatenate([part] * gp, axis=0),
                ROWS_BY_COLS,
                preferred_element_type=f32,
            )
            for part in (high, low)
        )
        place_of = lax.broadcasted_iota(jnp.int32, (uly, BLOCK), 1) // tok
        sums = jnp.where(place_of == lax.rem(u, gp), sums, 0.0)
        for h in range(uly):
            delta_send[h] = sums[h : h + 1]

    with jax.named_scope("send_gv"):
        for h, maybe_here in heads():
            ship(
                delta_send.at[h],
                delta_recv.at[b // 2, u],
                ds_sem.at[0],
                dr_sem.at[0],
                home(h, b),
                maybe_here,
            )
        z_send(GRAD)
        z_send(VALUE)

    def at(jb):
        return pl.ds(jb * BLOCK, BLOCK)

    def run_home(c):
        owned = [s for s in range(shards) if core_of(s) == c]
        foreign = [s for s in range(shards) if core_of(s) != c and s > owned[0]]
        lent = [s for s in owned if any(core_of(k) != c and k < s for k in range(shards))]
        tiles = [(q, k) for k in owned for q in range(k, shards)]
        slot = {tile: n for n, tile in enumerate(tiles)}
        q_all = sorted({q for q, _ in tiles})
        q_own = [q for q in q_all if q in owned]
        q_far = [q for q in q_all if q not in owned]
        pair_of = {QUERY: 0, GRAD: 1}
        wide = length // 2

        def own(t):
            with jax.named_scope(f"own_{t}"):
                for i in range(2):
                    n = lax.rem(u // (uly // 2) + i, 2)
                    for s in lent + [s for s in owned if s not in lent]:
                        ref = held.at[t, s, pl.ds(pl.multiple_of(n * wide, wide), wide), :]
                        remote(ref, ref, zs.at[0], zr.at[t, s // 2, n], (b, u)).wait_recv()
                        if t in pair_of and s in lent:
                            sem = sb.at[pair_of[t], s]
                            remote(ref, ref, sem, sem, sibling).start()

        def lent_copy(t, s):
            sem = sb.at[pair_of[t], s]
            return remote(held.at[t, s], held.at[t, s], sem, sem, sibling)

        turn = math.log2(math.e) * scale

        def keys_for(q, k, a):
            return (a + 1) * wide if q == k else length

        def first_lane(q, k, r):
            return r * wide if q == k else 0

        def lanes(a):
            return pl.ds(a * wide, wide)

        def fold(tile, op):
            return op(tile.reshape(tile.shape[0] // 8, 8, tile.shape[1]), axis=0)

        def bias_row(q, k, n, a):
            return bias[q, pl.ds(k * per + n, 1), lanes(a)]

        def make_scores(q, k, tops):
            new = []
            with jax.named_scope(f"scores_{q}_{k}"):
                for a in range(2):
                    count = keys_for(q, k, a)
                    tile = lax.dot_general(
                        held[KEY, k, :count, :],
                        held[QUERY, q, lanes(a), :],
                        ROWS_BY_COLS,
                        preferred_element_type=f32,
                    )
                    if q == k:
                        key_at = lax.broadcasted_iota(jnp.int32, (wide, wide), 0)
                        query_at = lax.broadcasted_iota(jnp.int32, (wide, wide), 1)
                        last = jnp.where(key_at <= query_at, tile[a * wide :], NEG)
                        tile = jnp.concatenate([tile[: a * wide], last], axis=0) if a else last
                    scores[slot[q, k], :count, lanes(a)] = tile
                    top = tops[a] if tops else None
                    for n in range(count // BLOCK):
                        part = fold(tile[n * BLOCK : (n + 1) * BLOCK], jnp.max)
                        part = part * turn + bias_row(q, k, n, a)
                        top = part if top is None else jnp.maximum(top, part)
                    new.append(top)
            return new

        def make_exps(q, tops):
            totals = []
            with jax.named_scope(f"exps_{q}"):
                for a in range(2):
                    top = jnp.max(tops[a], axis=0, keepdims=True)
                    total = jnp.zeros((8, wide), f32)
                    for k in owned:
                        if k > q:
                            continue
                        for n in range(keys_for(q, k, a) // BLOCK):
                            shift = top - bias_row(q, k, n, a)
                            tile = scores[slot[q, k], at(n), lanes(a)]
                            tile = jnp.exp2(tile * turn - shift)
                            scores[slot[q, k], at(n), lanes(a)] = tile
                            total = total + fold(tile, jnp.sum)
                    total = jnp.sum(total, axis=0, keepdims=True)
                    if q in lent or q in q_far:
                        stats[c, q, 0:1, lanes(a)] = top
                        stats[c, q, 1:2, lanes(a)] = total
                    totals.append(total)
            return jnp.concatenate(totals, axis=1)

        def pieces_of(q, k, start, stop):
            if q == k and start < wide < stop:
                return ((start, wide, 0), (wide, stop, wide))
            return ((start, stop, wide if q == k and start >= wide else 0),)

        def make_probs(q, k, start, stop, factor):
            with jax.named_scope(f"probs_{q}_{k}"):
                for low, high, first in pieces_of(q, k, start, stop):
                    probs = scores[slot[q, k], low:high, first:] * factor[:, first:]
                    probs_low[slot[q, k], low:high, first:] = probs.astype(jnp.bfloat16)

        def add(ref, value, fresh):
            if fresh:
                ref[...] = value
            else:
                ref[...] += value

        def make_values(q, k, start, stop, fresh):
            with jax.named_scope(f"values_{q}_{k}"):
                for low, high, first in pieces_of(q, k, start, stop):
                    product = jnp.dot(
                        probs_low[slot[q, k], low:high, first:],
                        held[GRAD, q, first:, :],
                        preferred_element_type=f32,
                    )
                    add(acc.at[D_VALUE, k, low:high, :], product, fresh)

        def make_grads(q, k, factor, delta):
            with jax.named_scope(f"grads_{q}_{k}"):
                for a in range(2):
                    count = keys_for(q, k, a)
                    prob_grad = lax.dot_general(
                        held[VALUE, k, :count, :],
                        held[GRAD, q, lanes(a), :],
                        ROWS_BY_COLS,
                        preferred_element_type=f32,
                    )
                    span = slice(a * wide, (a + 1) * wide)
                    grads = (scores[slot[q, k], :count, lanes(a)] * factor[:, span]) * (
                        prob_grad - delta[:, span]
                    )
                    score_grads[:count, lanes(a)] = grads.astype(jnp.bfloat16)

        def add_query(q, k, a, fresh):
            count = keys_for(q, k, a)
            product = lax.dot_general(
                score_grads[:count, lanes(a)],
                held[KEY, k, :count, :],
                COLS_BY_COLS,
                preferred_element_type=f32,
            )
            add(acc.at[D_QUERY, q, lanes(a), :], product, fresh)

        def add_key(q, k, r, fresh):
            first = first_lane(q, k, r)
            product = jnp.dot(
                score_grads[lanes(r), first:],
                held[QUERY, q, first:, :],
                preferred_element_type=f32,
            )
            add(acc.at[D_KEY, k, lanes(r), :], product, fresh)

        def send_result(t, s, start=0, stop=length):
            with jax.named_scope(f"send_{t}_{s}_{start}"):
                outgoing[t, s // 2, start:stop, :] = acc[t, s, start:stop, :].astype(jnp.bfloat16)
                inner, outer = 2 * base, 2 * (base + planes)
                targets = [(p, False) for p in range(uly) if not inner <= p < outer]
                for mask in reversed(range(outer - inner)):
                    p = inner + flip(u - inner, mask, outer - inner)
                    targets.append((p, mask == 0))
                for p, maybe_here in targets[start // tok : stop // tok]:
                    ship(
                        outgoing.at[t, s // 2, rows(p), :],
                        out_ref.at[t, :, cols(head)],
                        os_sem.at[0],
                        or_sem.at[0],
                        (s, p),
                        maybe_here,
                    )

        own(KEY)
        own(QUERY)
        tops, totals = {}, {}

        def all_scores(q):
            for k in owned:
                if k <= q:
                    tops[q] = make_scores(q, k, tops.get(q))
            totals[q] = make_exps(q, tops[q])

        for q in lent + q_far:
            if q in q_far:
                with jax.named_scope("lent_q"):
                    lent_copy(QUERY, q).wait_recv()
            all_scores(q)
        with jax.named_scope("stats"):
            remote(delta_recv, delta_recv, ds_sem.at[0], dr_sem.at[0], (b, u)).wait_recv()
            for s in owned:
                pieces = []
                for n in range(per):
                    piece = delta_recv[s // 2, n * gp]
                    for i in range(1, gp):
                        piece = piece + delta_recv[s // 2, n * gp + i]
                    pieces.append(piece)
                stats[c, s, 2:3, :] = jnp.concatenate(pieces, axis=1)
            remote(stats.at[c], stats.at[c], st.at[c], st.at[c], sibling).start()
        for q in q_own:
            if q not in lent:
                all_scores(q)
        own(GRAD)
        with jax.named_scope("stats_wait"):
            remote(stats.at[1 - c], stats.at[1 - c], st.at[c], st.at[1 - c], sibling).wait_recv()
        factors, deltas = {}, {}
        for q in q_all:
            if q in lent or q in q_far:
                top, total = stats[c, q, 0:1, :], stats[c, q, 1:2, :]
                top_far, total_far = stats[1 - c, q, 0:1, :], stats[1 - c, q, 1:2, :]
                high = jnp.maximum(top, top_far)
                share = jnp.exp2(top - high)
                factors[q] = share / (share * total + jnp.exp2(top_far - high) * total_far)
            else:
                factors[q] = 1.0 / totals[q]
            deltas[q] = stats[c if q in owned else 1 - c, q, 2:3, :]
        started = set()

        def starts(*what):
            new = what not in started
            started.add(what)
            return new

        have = set(q_own)
        early = min(tok * 2 * base, wide) if c == core_of(0) else 0
        spans = [(0, early), (early, length)] if early else [(0, length)]
        for start, stop in spans:
            for k in owned:
                queries = [q for q in q_own + q_far if q >= k]
                for q in queries:
                    make_probs(q, k, start, stop, factors[q])
                    if q not in have:
                        with jax.named_scope("lent_g"):
                            lent_copy(GRAD, q).wait_recv()
                        have.add(q)
                    make_values(q, k, start, stop, q == queries[0])
                send_result(D_VALUE, k, start, stop)
        own(VALUE)
        todo = [tile for tile in FIRST_TILES if tile in tiles]
        todo += [tile for tile in tiles if tile not in todo]
        waiting = []

        def finish_queries():
            while waiting:
                q = waiting.pop(0)
                with jax.named_scope(f"partial_{q}"):
                    ref = partial.at[q]
                    remote(ref, ref, pt.at[q], pt.at[q], sibling).wait_recv()
                    acc[D_QUERY, q] += partial[q]
                send_result(D_QUERY, q)

        while todo:
            q, k = todo.pop(0)
            make_grads(q, k, factors[q] * scale, deltas[q])
            fresh_query, fresh_key = starts("q", q), starts("k", k)
            with jax.named_scope(f"dots_{q}_{k}"):
                for a in range(2):
                    add_query(q, k, a, fresh_query)
                for r in range(2):
                    add_key(q, k, r, fresh_key)
            finish_queries()
            if all(tile[0] != q for tile in todo):
                if q in q_far:
                    ref = acc.at[D_QUERY, q]
                    remote(ref, partial.at[q], pt.at[q], pt.at[q], sibling).start()
                elif q in lent:
                    waiting.append(q)
                else:
                    send_result(D_QUERY, q)
            if all(tile[1] != k for tile in todo):
                send_result(D_KEY, k)
        finish_queries()
        with jax.named_scope("lent_sent"):
            for s in lent:
                for t in pair_of:
                    lent_copy(t, s).wait_send()
            for q in q_far:
                ref = acc.at[D_QUERY, q]
                remote(ref, ref, pt.at[q], pt.at[q], sibling).wait_send()
            remote(stats.at[c], stats.at[c], st.at[c], st.at[c], sibling).wait_send()

    @pl.when(is_home)
    def _():
        with jax.named_scope("bias"):
            lane_block = lax.broadcasted_iota(jnp.int32, (1, length), 1) // BLOCK
            key_block = lax.broadcasted_iota(jnp.int32, (blocks, length), 0)
            for s in range(shards):
                query_block = lane_block + s * per
                hit = (key_block == query_block) | (key_block == query_block - 1)
                hit = hit | (key_block == 0)
                for r in range(RAND):
                    named = jnp.zeros((1, length), jnp.int32)
                    for i in range(per):
                        named = jnp.where(lane_block == i, picks_ref[r, s * per + i], named)
                    hit = hit | (key_block == named)
                hit = hit & (key_block <= query_block)
                bias[s] = jnp.where(hit, 0.0, NEG)
        for c in range(2):
            pl.when(core == c)(functools.partial(run_home, c))

    def drain(count):
        ref = held.at[:, 0, pl.ds(0, count * tok), :]
        remote(ref, ref, zs.at[0], zr.at[0, 0, 0], (b, u)).wait_send()
        ref = delta_send.at[pl.ds(0, count)]
        remote(ref, ref, ds_sem.at[0], dr_sem.at[0], (b, u)).wait_send()

    with jax.named_scope("sent"):
        pl.when(own_source)(lambda: drain(uly - 1))
        pl.when(jnp.logical_not(own_source))(lambda: drain(uly))

        @pl.when(own_source)
        def _():
            ref = outgoing.at[:, :, pl.ds(0, length - tok // (shards // 2)), :]
            remote(ref, ref, os_sem.at[0], or_sem.at[0], (b, u)).wait_send()

        @pl.when(jnp.logical_and(is_home, jnp.logical_not(own_source)))
        def _():
            remote(outgoing, outgoing, os_sem.at[0], or_sem.at[0], (b, u)).wait_send()

    with jax.named_scope("landed"):
        remote(out_ref, out_ref, os_sem.at[0], or_sem.at[0], (b, u)).wait_recv()


def write_out(held, a_out, b_out, c_out, done):
    writes = [
        pltpu.make_async_copy(held.at[i], target, done.at[i])
        for i, target in enumerate((a_out, b_out, c_out))
    ]
    for write in writes:
        write.start()
    for write in writes:
        write.wait()


def fused_on_device(shards, uly, q, k, v, o, g, random_blocks):
    tok, width = q.shape
    length = tok * uly
    per = length // BLOCK
    half = shards // 2
    tiles = max(
        sum(shards - k for k in range(shards) if core_of(k) == core) for core in range(2)
    )
    dma = pltpu.SemaphoreType.DMA
    hbm = pl.BlockSpec(memory_space=pltpu.HBM)
    vmem = pl.BlockSpec(memory_space=pltpu.VMEM)
    placed = [
        pltpu.with_memory_space_constraint(x, pltpu.HBM) for x in (random_blocks.T, q, k, v, o, g)
    ]
    results = pl.pallas_call(
        functools.partial(fused_kernel, shards, uly),
        out_shape=jax.ShapeDtypeStruct((3, tok, width), jnp.bfloat16),
        in_specs=[hbm] * 6,
        out_specs=vmem,
        scratch_shapes=[
            pltpu.SMEM(random_blocks.shape[::-1], jnp.int32),
            pltpu.VMEM((2, tok, width), jnp.bfloat16),
            pltpu.VMEM((4, shards, length, HD), jnp.bfloat16),
            pltpu.VMEM((uly, 1, BLOCK), jnp.float32),
            pltpu.VMEM((half, uly, 1, BLOCK), jnp.float32),
            pltpu.VMEM((shards, shards * per, length), jnp.float32),
            pltpu.VMEM((2, shards, 3, length), jnp.float32),
            pltpu.VMEM((tiles, length, length), jnp.float32),
            pltpu.VMEM((tiles, length, length), jnp.bfloat16),
            pltpu.VMEM((length, length), jnp.bfloat16),
            pltpu.VMEM((3, shards, length, HD), jnp.float32),
            pltpu.VMEM((shards, length, HD), jnp.float32),
            pltpu.VMEM((3, half, length, HD), jnp.bfloat16),
            dma((1,)),
            dma((4, half, 2)),
            dma((2, shards)),
            dma((2,)),
            dma((shards,)),
            dma((1,)),
            dma((1,)),
            dma((1,)),
            dma((1,)),
            dma((3,)),
        ],
        compiler_params=pltpu.CompilerParams(
            collective_id=0, has_side_effects=True, vmem_limit_bytes=32 * 1024 * 1024
        ),
    )(*placed)
    return pl.pallas_call(
        write_out,
        out_shape=[jax.ShapeDtypeStruct((tok, width), jnp.bfloat16)] * 3,
        in_specs=[vmem],
        out_specs=[hbm] * 3,
        scratch_shapes=[dma((3,))],
        compiler_params=pltpu.CompilerParams(vmem_limit_bytes=32 * 1024 * 1024),
    )(results)


def wide_or_fused(shards, uly, *operands):
    tok, width = operands[0].shape
    length = tok * uly
    fits = shards * length * length * 4 <= 4 * 1024 * 1024
    paired = shards % 4 == 0 and uly % shards == 0
    if fits and paired and width == uly * HD and BLOCK % tok == 0 and length % BLOCK == 0:
        return tuple(fused_on_device(shards, uly, *operands))
    return on_device(*operands)


def solution(mesh):
    return jax.shard_map(
        functools.partial(wide_or_fused, mesh.shape["blk"], mesh.shape["uly"]),
        mesh=mesh,
        in_specs=(
            P(("blk", "uly"), None),
            P(("blk", "uly"), None),
            P(("blk", "uly"), None),
            P(("blk", "uly"), None),
            P(("blk", "uly"), None),
            P(),
        ),
        out_specs=(P(("blk", "uly"), None), P(("blk", "uly"), None), P(("blk", "uly"), None)),
        check_vma=False,
    )
```

```python
import functools
import math

import jax
import jax.numpy as jnp
from jax import lax
from jax.experimental import pallas as pl
from jax.experimental.pallas import tpu as pltpu
from jax.sharding import PartitionSpec as P

HD = 128
BLOCK = 128
RAND = 3
CAP = 2


def named_table(random_blocks, per_shard):
    block_count = random_blocks.shape[0]
    shard_count = block_count // per_shard
    entries = random_blocks.reshape(shard_count, per_shard * RAND)
    block_ids = jnp.arange(block_count, dtype=jnp.int32)
    named = jnp.any(entries[:, :, None] == block_ids[None, None, :], axis=1)
    owner = block_ids // per_shard
    named = named & (owner[None, :] != jnp.arange(shard_count, dtype=jnp.int32)[:, None])
    grouped = named.reshape(shard_count, shard_count, per_shard).astype(jnp.int32)
    rank_in = jnp.cumsum(grouped, axis=2) - grouped
    return (grouped, rank_in)


def send_slots(grouped, rank_in, cycle_rank, per_shard):
    mine = lax.dynamic_index_in_dim(grouped, cycle_rank, 1, keepdims=False)
    mine_rank = lax.dynamic_index_in_dim(rank_in, cycle_rank, 1, keepdims=False)
    slot_ids = jnp.arange(CAP, dtype=jnp.int32)
    hit = (mine[:, None, :] == 1) & (mine_rank[:, None, :] == slot_ids[None, :, None])
    positions = jnp.arange(per_shard, dtype=jnp.int32)
    select = jnp.sum(jnp.where(hit, positions[None, None, :], 0), axis=2)
    filled = jnp.any(hit, axis=2)
    return (select, filled)


def on_device(query_proj, key_proj, value_proj, attn_output, out_grad, random_blocks):
    tok_count = query_proj.shape[0]
    head_count = query_proj.shape[1] // HD
    score_scale = HD ** (-0.5)
    extent = 3 + RAND

    def to_heads(tensor):
        return tensor.reshape(tok_count, head_count, HD)

    query_rows, key_rows, value_rows, output_rows, grad_rows = (
        lax.all_to_all(to_heads(query_proj), "uly", split_axis=1, concat_axis=0, tiled=True),
        lax.all_to_all(to_heads(key_proj), "uly", split_axis=1, concat_axis=0, tiled=True),
        lax.all_to_all(to_heads(value_proj), "uly", split_axis=1, concat_axis=0, tiled=True),
        lax.all_to_all(to_heads(attn_output), "uly", split_axis=1, concat_axis=0, tiled=True),
        lax.all_to_all(to_heads(out_grad), "uly", split_axis=1, concat_axis=0, tiled=True),
    )
    row_delta = jnp.sum(
        output_rows.astype(jnp.float32) * grad_rows.astype(jnp.float32), axis=2
    ).reshape(-1)
    shard_len = query_rows.shape[0]
    per_shard = shard_len // BLOCK
    query_blocks = query_rows.reshape(per_shard, BLOCK, HD)
    key_blocks = key_rows.reshape(per_shard, BLOCK, HD)
    value_blocks = value_rows.reshape(per_shard, BLOCK, HD)
    grad_blocks = grad_rows.reshape(per_shard, BLOCK, HD)
    delta_blocks = row_delta.reshape(per_shard, BLOCK)
    cycle_size = lax.axis_size("blk")
    cycle_rank = lax.axis_index("blk")
    block_count = random_blocks.shape[0]
    grouped, rank_in = named_table(random_blocks, per_shard)
    select, filled = send_slots(grouped, rank_in, cycle_rank, per_shard)
    key_send = jnp.where(
        filled[:, :, None, None],
        jnp.take(key_blocks, select.reshape(-1), axis=0).reshape(cycle_size, CAP, BLOCK, HD),
        jnp.zeros((), jnp.bfloat16),
    )
    value_send = jnp.where(
        filled[:, :, None, None],
        jnp.take(value_blocks, select.reshape(-1), axis=0).reshape(cycle_size, CAP, BLOCK, HD),
        jnp.zeros((), jnp.bfloat16),
    )
    extra_key = jnp.broadcast_to(
        jnp.stack([key_blocks[per_shard - 1], key_blocks[0]])[None], (cycle_size, 2, BLOCK, HD)
    )
    extra_value = jnp.broadcast_to(
        jnp.stack([value_blocks[per_shard - 1], value_blocks[0]])[None], (cycle_size, 2, BLOCK, HD)
    )
    all_key, all_value = (
        lax.all_to_all(
            jnp.concatenate([key_send, extra_key], axis=1),
            "blk",
            split_axis=0,
            concat_axis=0,
            tiled=True,
        ),
        lax.all_to_all(
            jnp.concatenate([value_send, extra_value], axis=1),
            "blk",
            split_axis=0,
            concat_axis=0,
            tiled=True,
        ),
    )
    far_key = all_key[:, :CAP]
    far_value = all_value[:, :CAP]
    before_rank = jnp.maximum(cycle_rank - 1, 0)
    prev_key = lax.dynamic_index_in_dim(all_key, before_rank, 0, keepdims=False)[CAP]
    prev_value = lax.dynamic_index_in_dim(all_value, before_rank, 0, keepdims=False)[CAP]
    first_key = all_key[0, CAP + 1]
    first_value = all_value[0, CAP + 1]
    key_store = jnp.concatenate(
        [key_blocks, prev_key[None], first_key[None], far_key.reshape(cycle_size * CAP, BLOCK, HD)],
        axis=0,
    )
    value_store = jnp.concatenate(
        [
            value_blocks,
            prev_value[None],
            first_value[None],
            far_value.reshape(cycle_size * CAP, BLOCK, HD),
        ],
        axis=0,
    )
    store_size = key_store.shape[0]
    picked = lax.dynamic_slice_in_dim(random_blocks, cycle_rank * per_shard, per_shard, 0)
    own_rank = lax.dynamic_index_in_dim(rank_in, cycle_rank, 0, keepdims=False).reshape(-1)
    all_ids = jnp.arange(block_count, dtype=jnp.int32)
    slot_of = jnp.sum(
        jnp.where(picked[:, :, None] == all_ids[None, None, :], own_rank[None, None, :], 0), axis=2
    )
    owner = picked // per_shard
    random_index = jnp.where(
        owner == cycle_rank, picked - cycle_rank * per_shard, per_shard + 2 + owner * CAP + slot_of
    )
    local_ids = jnp.arange(per_shard, dtype=jnp.int32)
    global_ids = cycle_rank * per_shard + local_ids
    listed = jnp.concatenate(
        [
            global_ids[:, None],
            global_ids[:, None] - 1,
            jnp.zeros((per_shard, 1), jnp.int32),
            picked,
        ],
        axis=1,
    )
    first_index = jnp.zeros((per_shard, 1), jnp.int32) + jnp.where(
        cycle_rank == 0, 0, per_shard + 1
    ).astype(jnp.int32)
    store_index = jnp.concatenate(
        [
            local_ids[:, None],
            jnp.where(local_ids >= 1, local_ids - 1, per_shard)[:, None],
            first_index,
            random_index,
        ],
        axis=1,
    )
    order = jnp.arange(extent, dtype=jnp.int32)
    earlier = order[None, :] < order[:, None]
    repeated = jnp.any((listed[:, :, None] == listed[:, None, :]) & earlier[None, :, :], axis=2)
    usable = (listed >= 0) & jnp.logical_not(repeated)
    within = jnp.arange(BLOCK, dtype=jnp.int32)
    group = math.gcd(per_shard, max(1, 512 // BLOCK))
    group_count = per_shard // group

    def group_turn(carry, group_index):
        key_grad_store, value_grad_store = carry
        first = group_index * group
        query_grp = lax.dynamic_slice_in_dim(query_blocks, first, group, 0)
        grad_grp = lax.dynamic_slice_in_dim(grad_blocks, first, group, 0)
        delta_grp = lax.dynamic_slice_in_dim(delta_blocks, first, group, 0)
        index_grp = lax.dynamic_slice_in_dim(store_index, first, group, 0).reshape(-1)
        listed_grp = lax.dynamic_slice_in_dim(listed, first, group, 0)
        usable_grp = lax.dynamic_slice_in_dim(usable, first, group, 0)
        key_sel = jnp.take(key_store, index_grp, axis=0).reshape(group, extent * BLOCK, HD)
        value_sel = jnp.take(value_store, index_grp, axis=0).reshape(group, extent * BLOCK, HD)
        scores = (
            jnp.einsum("gqd,gkd->gqk", query_grp, key_sel, preferred_element_type=jnp.float32)
            * score_scale
        )
        query_pos = (cycle_rank * per_shard + first + jnp.arange(group, dtype=jnp.int32))[
            :, None
        ] * BLOCK + within[None, :]
        key_pos = (listed_grp[:, :, None] * BLOCK + within[None, None, :]).reshape(
            group, extent * BLOCK
        )
        allowed = jnp.repeat(usable_grp, BLOCK, axis=1)[:, None, :] & (
            key_pos[:, None, :] <= query_pos[:, :, None]
        )
        row_max = jnp.max(jnp.where(allowed, scores, -1e30), axis=2)
        total = jnp.sum(jnp.where(allowed, jnp.exp(scores - row_max[:, :, None]), 0.0), axis=2)
        log_total = row_max + jnp.log(total)
        probs = jnp.where(allowed, jnp.exp(scores - log_total[:, :, None]), 0.0)
        prob_grad = jnp.einsum(
            "gqd,gkd->gqk", grad_grp, value_sel, preferred_element_type=jnp.float32
        )
        score_grad = (probs * (prob_grad - delta_grp[:, :, None]) * score_scale).astype(
            jnp.bfloat16
        )
        query_part = jnp.einsum(
            "gqk,gkd->gqd", score_grad, key_sel, preferred_element_type=jnp.float32
        ).astype(jnp.bfloat16)
        key_part = jnp.einsum(
            "gqk,gqd->gkd", score_grad, query_grp, preferred_element_type=jnp.float32
        )
        value_part = jnp.einsum(
            "gqk,gqd->gkd", probs.astype(jnp.bfloat16), grad_grp, preferred_element_type=jnp.float32
        )
        key_grad_store = key_grad_store.at[index_grp].add(
            key_part.reshape(group * extent, BLOCK, HD)
        )
        value_grad_store = value_grad_store.at[index_grp].add(
            value_part.reshape(group * extent, BLOCK, HD)
        )
        return ((key_grad_store, value_grad_store), query_part)

    zero_store = jnp.zeros((store_size, BLOCK, HD), jnp.float32)
    (key_grad_store, value_grad_store), query_parts = lax.scan(
        group_turn, (zero_store, zero_store), jnp.arange(group_count, dtype=jnp.int32)
    )
    query_acc = query_parts.reshape(shard_len, HD)
    key_acc = key_grad_store[:per_shard]
    value_acc = value_grad_store[:per_shard]
    far_key_grad = key_grad_store[per_shard + 2 :].reshape(cycle_size, CAP, BLOCK, HD)
    far_value_grad = value_grad_store[per_shard + 2 :].reshape(cycle_size, CAP, BLOCK, HD)
    dest_ids = jnp.arange(cycle_size, dtype=jnp.int32)
    to_prev = (dest_ids == cycle_rank - 1)[:, None, None]
    to_first = (dest_ids == 0)[:, None, None]
    extra_key_grad = jnp.stack(
        [
            jnp.where(to_prev, key_grad_store[per_shard][None], 0.0),
            jnp.where(to_first, key_grad_store[per_shard + 1][None], 0.0),
        ],
        axis=1,
    )
    extra_value_grad = jnp.stack(
        [
            jnp.where(to_prev, value_grad_store[per_shard][None], 0.0),
            jnp.where(to_first, value_grad_store[per_shard + 1][None], 0.0),
        ],
        axis=1,
    )
    all_key_back, all_value_back = (
        lax.all_to_all(
            jnp.concatenate([far_key_grad, extra_key_grad], axis=1),
            "blk",
            split_axis=0,
            concat_axis=0,
            tiled=True,
        ),
        lax.all_to_all(
            jnp.concatenate([far_value_grad, extra_value_grad], axis=1),
            "blk",
            split_axis=0,
            concat_axis=0,
            tiled=True,
        ),
    )
    back_key = all_key_back[:, :CAP]
    back_value = all_value_back[:, :CAP]
    prev_back = jnp.stack(
        [jnp.sum(all_key_back[:, CAP], axis=0), jnp.sum(all_value_back[:, CAP], axis=0)]
    )
    first_back = jnp.stack(
        [jnp.sum(all_key_back[:, CAP + 1], axis=0), jnp.sum(all_value_back[:, CAP + 1], axis=0)]
    )
    key_acc = key_acc.at[per_shard - 1].add(prev_back[0]).at[0].add(first_back[0])
    value_acc = value_acc.at[per_shard - 1].add(prev_back[1]).at[0].add(first_back[1])
    back_key = jnp.where(filled[:, :, None, None], back_key, 0.0).reshape(
        cycle_size * CAP, BLOCK, HD
    )
    back_value = jnp.where(filled[:, :, None, None], back_value, 0.0).reshape(
        cycle_size * CAP, BLOCK, HD
    )
    key_acc = key_acc.at[select.reshape(-1)].add(back_key).reshape(shard_len, HD)
    value_acc = value_acc.at[select.reshape(-1)].add(back_value).reshape(shard_len, HD)
    outgoing = (
        query_acc.reshape(shard_len, 1, HD),
        key_acc.astype(jnp.bfloat16).reshape(shard_len, 1, HD),
        value_acc.astype(jnp.bfloat16).reshape(shard_len, 1, HD),
    )
    query_back, key_back, value_back = (
        lax.all_to_all(outgoing[0], "uly", split_axis=0, concat_axis=1, tiled=True),
        lax.all_to_all(outgoing[1], "uly", split_axis=0, concat_axis=1, tiled=True),
        lax.all_to_all(outgoing[2], "uly", split_axis=0, concat_axis=1, tiled=True),
    )
    return (
        query_back.reshape(tok_count, head_count * HD),
        key_back.reshape(tok_count, head_count * HD),
        value_back.reshape(tok_count, head_count * HD),
    )


NEG = -1e30
KEY, QUERY, GRAD, VALUE = 0, 1, 2, 3
D_QUERY, D_KEY, D_VALUE = 0, 1, 2
ROWS_BY_COLS = (((1,), (1,)), ((), ()))
COLS_BY_COLS = (((0,), (0,)), ((), ()))


FIRST_TILES = ((0, 0), (1, 0), (2, 0), (3, 0), (3, 3), (3, 2), (3, 1), (2, 2), (1, 1), (2, 1))


def flip(value, mask, count):
    if count & (count - 1):
        return lax.rem(value + mask, count)
    for bit in range(count.bit_length() - 1):
        if mask >> bit & 1:
            value = value + (1 << bit) * (1 - 2 * (value // (1 << bit) % 2))
    return value


def core_of(shard):
    return (shard + 1) // 2 % 2


def fused_kernel(
    shards,
    uly,
    picks_hbm,
    q_ref,
    k_ref,
    v_ref,
    o_ref,
    g_ref,
    out_ref,
    picks_ref,
    rows_in,
    held,
    delta_send,
    delta_recv,
    bias,
    stats,
    scores,
    probs_low,
    score_grads,
    acc,
    partial,
    outgoing,
    zs,
    zr,
    sb,
    st,
    pt,
    ds_sem,
    dr_sem,
    os_sem,
    or_sem,
    il,
):
    tok = q_ref.shape[0]
    length = tok * uly
    per = length // BLOCK
    gp = BLOCK // tok
    blocks = per * shards
    planes = uly // shards
    base = (uly // 2 - planes) // 2
    scale = HD ** (-0.5)
    f32 = jnp.float32
    b = lax.axis_index("blk")
    u = lax.axis_index("uly")
    uz, core = u // 2, u % 2
    plane = uz - base
    is_home = jnp.logical_and(plane >= 0, plane < planes)
    near = jnp.clip(plane, 0, planes - 1)
    head = b + shards * near
    own_source = jnp.logical_and(is_home, core_of(b) == core)
    inputs = {KEY: k_ref, QUERY: q_ref, VALUE: v_ref, GRAD: g_ref}
    mesh_ids = pl.DeviceIdType.MESH

    def home(h, s):
        return h % shards, (base + h // shards) * 2 + core_of(s)

    sibling = (b, uz * 2 + 1 - core)

    def is_self(place):
        return jnp.logical_and(place[0] == b, place[1] == u)

    def ids(place):
        return {"blk": place[0], "uly": place[1]}

    def cols(p):
        return pl.ds(pl.multiple_of(p * HD, HD), HD)

    def rows(p):
        return pl.ds(pl.multiple_of(p * tok, tok), tok)

    def remote(source, target, send, recv, place):
        return pltpu.make_async_remote_copy(
            src_ref=source,
            dst_ref=target,
            send_sem=send,
            recv_sem=recv,
            device_id=ids(place),
            device_id_type=mesh_ids,
        )

    def ship(source, target, send, recv, place, maybe_here):
        if not maybe_here:
            remote(source, target, send, recv, place).start()
            return
        mine = is_self(place)

        @pl.when(jnp.logical_not(mine))
        def _():
            remote(source, target, send, recv, place).start()

        @pl.when(mine)
        def _():
            pltpu.make_async_copy(source, target, recv).start()

    def heads():
        return [(flip(head, mask, uly), mask == 0) for mask in reversed(range(uly))]

    def z_send(t):
        for h, maybe_here in heads():
            ship(
                inputs[t].at[:, cols(h)],
                held.at[t, b, rows(u), :],
                zs.at[0],
                zr.at[t, b // 2, u // (uly // 2)],
                home(h, b),
                maybe_here,
            )

    fetches = (
        pltpu.make_async_copy(o_ref, rows_in.at[0], il.at[0]),
        pltpu.make_async_copy(g_ref, rows_in.at[1], il.at[1]),
        pltpu.make_async_copy(picks_hbm, picks_ref, il.at[2]),
    )
    barrier = pltpu.get_barrier_semaphore()

    def greet(place):
        pl.semaphore_signal(barrier, inc=1, device_id=ids(place), device_id_type=mesh_ids)

    with jax.named_scope("greet"):

        @pl.when(is_home)
        def _():
            for p in range(uly):
                for j in range(shards // 2):
                    place = (2 * j + (core + j) % 2, p)
                    pl.when(jnp.logical_not(is_self(place)))(functools.partial(greet, place))
            greet(sibling)

        for fetch in fetches:
            fetch.start()
    with jax.named_scope("barrier"):
        pl.semaphore_wait(
            barrier, uly - jnp.where(own_source, 1, 0) + jnp.where(is_home, 1, 0)
        )
    with jax.named_scope("send_kq"):
        z_send(KEY)
        z_send(QUERY)

    with jax.named_scope("prep"):
        for fetch in fetches:
            fetch.wait()
        product = rows_in[0].astype(f32) * rows_in[1].astype(f32)
        high = product.astype(jnp.bfloat16)
        low = (product - high.astype(f32)).astype(jnp.bfloat16)
        head_of = lax.broadcasted_iota(jnp.int32, (uly, uly * HD), 1) // HD
        pick_head = jnp.where(
            head_of == lax.broadcasted_iota(jnp.int32, (uly, uly * HD), 0), 1.0, 0.0
        ).astype(jnp.bfloat16)
        sums = sum(
            lax.dot_general(
                pick_head,
                jnp.concatenate([part] * gp, axis=0),
                ROWS_BY_COLS,
                preferred_element_type=f32,
            )
            for part in (high, low)
        )
        place_of = lax.broadcasted_iota(jnp.int32, (uly, BLOCK), 1) // tok
        sums = jnp.where(place_of == lax.rem(u, gp), sums, 0.0)
        for h in range(uly):
            delta_send[h] = sums[h : h + 1]

    with jax.named_scope("send_gv"):
        for h, maybe_here in heads():
            ship(
                delta_send.at[h],
                delta_recv.at[b // 2, u],
                ds_sem.at[0],
                dr_sem.at[0],
                home(h, b),
                maybe_here,
            )
        z_send(GRAD)
        z_send(VALUE)

    def at(jb):
        return pl.ds(jb * BLOCK, BLOCK)

    def run_home(c):
        owned = [s for s in range(shards) if core_of(s) == c]
        foreign = [s for s in range(shards) if core_of(s) != c and s > owned[0]]
        lent = [s for s in owned if any(core_of(k) != c and k < s for k in range(shards))]
        tiles = [(q, k) for k in owned for q in range(k, shards)]
        slot = {tile: n for n, tile in enumerate(tiles)}
        q_all = sorted({q for q, _ in tiles})
        q_own = [q for q in q_all if q in owned]
        q_far = [q for q in q_all if q not in owned]
        pair_of = {QUERY: 0, GRAD: 1}
        wide = length // 2

        def own(t):
            with jax.named_scope(f"own_{t}"):
                for i in range(2):
                    n = lax.rem(u // (uly // 2) + i, 2)
                    for s in lent + [s for s in owned if s not in lent]:
                        ref = held.at[t, s, pl.ds(pl.multiple_of(n * wide, wide), wide), :]
                        remote(ref, ref, zs.at[0], zr.at[t, s // 2, n], (b, u)).wait_recv()
                        if t in pair_of and s in lent:
                            sem = sb.at[pair_of[t], s]
                            remote(ref, ref, sem, sem, sibling).start()

        def lent_copy(t, s):
            sem = sb.at[pair_of[t], s]
            return remote(held.at[t, s], held.at[t, s], sem, sem, sibling)

        turn = math.log2(math.e) * scale

        def keys_for(q, k, a):
            return (a + 1) * wide if q == k else length

        def first_lane(q, k, r):
            return r * wide if q == k else 0

        def lanes(a):
            return pl.ds(a * wide, wide)

        def fold(tile, op):
            return op(tile.reshape(tile.shape[0] // 8, 8, tile.shape[1]), axis=0)

        def bias_row(q, k, n, a):
            return bias[q, pl.ds(k * per + n, 1), lanes(a)]

        def make_scores(q, k, tops):
            new = []
            with jax.named_scope(f"scores_{q}_{k}"):
                for a in range(2):
                    count = keys_for(q, k, a)
                    tile = lax.dot_general(
                        held[KEY, k, :count, :],
                        held[QUERY, q, lanes(a), :],
                        ROWS_BY_COLS,
                        preferred_element_type=f32,
                    )
                    if q == k:
                        key_at = lax.broadcasted_iota(jnp.int32, (wide, wide), 0)
                        query_at = lax.broadcasted_iota(jnp.int32, (wide, wide), 1)
                        last = jnp.where(key_at <= query_at, tile[a * wide :], NEG)
                        tile = jnp.concatenate([tile[: a * wide], last], axis=0) if a else last
                    scores[slot[q, k], :count, lanes(a)] = tile
                    top = tops[a] if tops else None
                    for n in range(count // BLOCK):
                        part = fold(tile[n * BLOCK : (n + 1) * BLOCK], jnp.max)
                        part = part * turn + bias_row(q, k, n, a)
                        top = part if top is None else jnp.maximum(top, part)
                    new.append(top)
            return new

        def make_exps(q, tops):
            totals = []
            with jax.named_scope(f"exps_{q}"):
                for a in range(2):
                    top = jnp.max(tops[a], axis=0, keepdims=True)
                    total = jnp.zeros((8, wide), f32)
                    for k in owned:
                        if k > q:
                            continue
                        for n in range(keys_for(q, k, a) // BLOCK):
                            shift = top - bias_row(q, k, n, a)
                            tile = scores[slot[q, k], at(n), lanes(a)]
                            tile = jnp.exp2(tile * turn - shift)
                            scores[slot[q, k], at(n), lanes(a)] = tile
                            total = total + fold(tile, jnp.sum)
                    total = jnp.sum(total, axis=0, keepdims=True)
                    if q in lent or q in q_far:
                        stats[c, q, 0:1, lanes(a)] = top
                        stats[c, q, 1:2, lanes(a)] = total
                    totals.append(total)
            return jnp.concatenate(totals, axis=1)

        def pieces_of(q, k, start, stop):
            if q == k and start < wide < stop:
                return ((start, wide, 0), (wide, stop, wide))
            return ((start, stop, wide if q == k and start >= wide else 0),)

        def make_probs(q, k, start, stop, factor):
            with jax.named_scope(f"probs_{q}_{k}"):
                for low, high, first in pieces_of(q, k, start, stop):
                    probs = scores[slot[q, k], low:high, first:] * factor[:, first:]
                    probs_low[slot[q, k], low:high, first:] = probs.astype(jnp.bfloat16)

        def add(ref, value, fresh, result=None):
            if not fresh:
                value = value + ref[...]
            if result is None:
                ref[...] = value
            else:
                result[...] = value.astype(jnp.bfloat16)

        def make_values(q, k, start, stop, fresh, last):
            with jax.named_scope(f"values_{q}_{k}"):
                for low, high, first in pieces_of(q, k, start, stop):
                    product = jnp.dot(
                        probs_low[slot[q, k], low:high, first:],
                        held[GRAD, q, first:, :],
                        preferred_element_type=f32,
                    )
                    result = outgoing.at[D_VALUE, k // 2, low:high, :] if last else None
                    add(acc.at[D_VALUE, k, low:high, :], product, fresh, result)

        def make_grads(q, k, factor, delta):
            with jax.named_scope(f"grads_{q}_{k}"):
                for a in range(2):
                    count = keys_for(q, k, a)
                    prob_grad = lax.dot_general(
                        held[VALUE, k, :count, :],
                        held[GRAD, q, lanes(a), :],
                        ROWS_BY_COLS,
                        preferred_element_type=f32,
                    )
                    span = slice(a * wide, (a + 1) * wide)
                    grads = (scores[slot[q, k], :count, lanes(a)] * factor[:, span]) * (
                        prob_grad - delta[:, span]
                    )
                    score_grads[:count, lanes(a)] = grads.astype(jnp.bfloat16)

        def add_query(q, k, a, fresh, last):
            count = keys_for(q, k, a)
            product = lax.dot_general(
                score_grads[:count, lanes(a)],
                held[KEY, k, :count, :],
                COLS_BY_COLS,
                preferred_element_type=f32,
            )
            result = outgoing.at[D_QUERY, q // 2, lanes(a), :] if last else None
            add(acc.at[D_QUERY, q, lanes(a), :], product, fresh, result)

        def add_key(q, k, r, fresh, last):
            first = first_lane(q, k, r)
            product = jnp.dot(
                score_grads[lanes(r), first:],
                held[QUERY, q, first:, :],
                preferred_element_type=f32,
            )
            result = outgoing.at[D_KEY, k // 2, lanes(r), :] if last else None
            add(acc.at[D_KEY, k, lanes(r), :], product, fresh, result)

        def send_result(t, s, start=0, stop=length):
            with jax.named_scope(f"send_{t}_{s}_{start}"):
                inner, outer = 2 * base, 2 * (base + planes)
                targets = [(p, False) for p in range(uly) if not inner <= p < outer]
                for mask in reversed(range(outer - inner)):
                    p = inner + flip(u - inner, mask, outer - inner)
                    targets.append((p, mask == 0))
                for p, maybe_here in targets[start // tok : stop // tok]:
                    ship(
                        outgoing.at[t, s // 2, rows(p), :],
                        out_ref.at[t, :, cols(head)],
                        os_sem.at[0],
                        or_sem.at[0],
                        (s, p),
                        maybe_here,
                    )

        own(KEY)
        own(QUERY)
        tops, totals = {}, {}

        def all_scores(queries):
            for q in queries:
                for k in owned:
                    if k <= q:
                        tops[q] = make_scores(q, k, tops.get(q))
            for q in queries:
                totals[q] = make_exps(q, tops[q])

        all_scores(lent if c else [])
        with jax.named_scope("lent_q"):
            for q in q_far:
                lent_copy(QUERY, q).wait_recv()
        all_scores(q_far if c else lent + q_far)
        with jax.named_scope("stats"):
            remote(delta_recv, delta_recv, ds_sem.at[0], dr_sem.at[0], (b, u)).wait_recv()
            for s in owned:
                pieces = []
                for n in range(per):
                    piece = delta_recv[s // 2, n * gp]
                    for i in range(1, gp):
                        piece = piece + delta_recv[s // 2, n * gp + i]
                    pieces.append(piece)
                stats[c, s, 2:3, :] = jnp.concatenate(pieces, axis=1)
            remote(stats.at[c], stats.at[c], st.at[c], st.at[c], sibling).start()
        all_scores([q for q in q_own if q not in lent])
        own(GRAD)
        with jax.named_scope("stats_wait"):
            remote(stats.at[1 - c], stats.at[1 - c], st.at[c], st.at[1 - c], sibling).wait_recv()
        factors, deltas = {}, {}
        for q in q_all:
            if q in lent or q in q_far:
                top, total = stats[c, q, 0:1, :], stats[c, q, 1:2, :]
                top_far, total_far = stats[1 - c, q, 0:1, :], stats[1 - c, q, 1:2, :]
                high = jnp.maximum(top, top_far)
                share = jnp.exp2(top - high)
                factors[q] = share / (share * total + jnp.exp2(top_far - high) * total_far)
            else:
                factors[q] = 1.0 / totals[q]
            deltas[q] = stats[c if q in owned else 1 - c, q, 2:3, :]
        started = set()

        def starts(*what):
            new = what not in started
            started.add(what)
            return new

        have = set(q_own)
        early = min(tok * 2 * base, wide) if c == core_of(0) else 0
        spans = [(0, early), (early, length)] if early else [(0, length)]
        for start, stop in spans:
            for k in owned:
                queries = [q for q in q_own + q_far if q >= k]
                for q in queries:
                    make_probs(q, k, start, stop, factors[q])
                    if q not in have:
                        with jax.named_scope("lent_g"):
                            lent_copy(GRAD, q).wait_recv()
                        have.add(q)
                    make_values(q, k, start, stop, q == queries[0], q == queries[-1])
                send_result(D_VALUE, k, start, stop)
        own(VALUE)
        todo = [tile for tile in FIRST_TILES if tile in tiles]
        todo += [tile for tile in tiles if tile not in todo]
        waiting = []

        def finish_queries():
            while waiting:
                q = waiting.pop(0)
                with jax.named_scope(f"partial_{q}"):
                    ref = partial.at[q]
                    remote(ref, ref, pt.at[q], pt.at[q], sibling).wait_recv()
                    total = acc[D_QUERY, q] + partial[q]
                    outgoing[D_QUERY, q // 2] = total.astype(jnp.bfloat16)
                send_result(D_QUERY, q)

        while todo:
            q, k = todo.pop(0)
            make_grads(q, k, factors[q] * scale, deltas[q])
            fresh_query, fresh_key = starts("q", q), starts("k", k)
            last_query = all(tile[0] != q for tile in todo)
            last_key = all(tile[1] != k for tile in todo)
            whole_query = last_query and q in q_own and q not in lent
            with jax.named_scope(f"dots_{q}_{k}"):
                for a in range(2):
                    add_query(q, k, a, fresh_query, whole_query)
                for r in range(2):
                    add_key(q, k, r, fresh_key, last_key)
            finish_queries()
            if last_query:
                if q in q_far:
                    ref = acc.at[D_QUERY, q]
                    remote(ref, partial.at[q], pt.at[q], pt.at[q], sibling).start()
                elif q in lent:
                    waiting.append(q)
                else:
                    send_result(D_QUERY, q)
            if last_key:
                send_result(D_KEY, k)
        finish_queries()
        with jax.named_scope("lent_sent"):
            for s in lent:
                for t in pair_of:
                    lent_copy(t, s).wait_send()
            for q in q_far:
                ref = acc.at[D_QUERY, q]
                remote(ref, ref, pt.at[q], pt.at[q], sibling).wait_send()
            remote(stats.at[c], stats.at[c], st.at[c], st.at[c], sibling).wait_send()

    @pl.when(is_home)
    def _():
        with jax.named_scope("bias"):
            lane_block = lax.broadcasted_iota(jnp.int32, (1, length), 1) // BLOCK
            key_block = lax.broadcasted_iota(jnp.int32, (blocks, length), 0)
            for s in range(shards):
                query_block = lane_block + s * per
                hit = (key_block == query_block) | (key_block == query_block - 1)
                hit = hit | (key_block == 0)
                for r in range(RAND):
                    named = jnp.zeros((1, length), jnp.int32)
                    for i in range(per):
                        named = jnp.where(lane_block == i, picks_ref[r, s * per + i], named)
                    hit = hit | (key_block == named)
                hit = hit & (key_block <= query_block)
                bias[s] = jnp.where(hit, 0.0, NEG)
        for c in range(2):
            pl.when(core == c)(functools.partial(run_home, c))

    def drain(count):
        ref = held.at[:, 0, pl.ds(0, count * tok), :]
        remote(ref, ref, zs.at[0], zr.at[0, 0, 0], (b, u)).wait_send()
        ref = delta_send.at[pl.ds(0, count)]
        remote(ref, ref, ds_sem.at[0], dr_sem.at[0], (b, u)).wait_send()

    with jax.named_scope("sent"):
        pl.when(own_source)(lambda: drain(uly - 1))
        pl.when(jnp.logical_not(own_source))(lambda: drain(uly))

        @pl.when(own_source)
        def _():
            ref = outgoing.at[:, :, pl.ds(0, length - tok // (shards // 2)), :]
            remote(ref, ref, os_sem.at[0], or_sem.at[0], (b, u)).wait_send()

        @pl.when(jnp.logical_and(is_home, jnp.logical_not(own_source)))
        def _():
            remote(outgoing, outgoing, os_sem.at[0], or_sem.at[0], (b, u)).wait_send()

    with jax.named_scope("landed"):
        remote(out_ref, out_ref, os_sem.at[0], or_sem.at[0], (b, u)).wait_recv()


def write_out(held, a_out, b_out, c_out, done):
    half = held.shape[1] // 2
    writes = [
        pltpu.make_async_copy(
            held.at[i, pl.ds(n * half, half)], target.at[pl.ds(n * half, half)], done.at[2 * i + n]
        )
        for i, target in enumerate((a_out, b_out, c_out))
        for n in range(2)
    ]
    for write in writes:
        write.start()
    for write in writes:
        write.wait()


def fused_on_device(shards, uly, q, k, v, o, g, random_blocks):
    tok, width = q.shape
    length = tok * uly
    per = length // BLOCK
    half = shards // 2
    tiles = max(
        sum(shards - k for k in range(shards) if core_of(k) == core) for core in range(2)
    )
    dma = pltpu.SemaphoreType.DMA
    hbm = pl.BlockSpec(memory_space=pltpu.HBM)
    vmem = pl.BlockSpec(memory_space=pltpu.VMEM)
    placed = [
        pltpu.with_memory_space_constraint(x, pltpu.HBM) for x in (random_blocks.T, q, k, v, o, g)
    ]
    results = pl.pallas_call(
        functools.partial(fused_kernel, shards, uly),
        out_shape=jax.ShapeDtypeStruct((3, tok, width), jnp.bfloat16),
        in_specs=[hbm] * 6,
        out_specs=vmem,
        scratch_shapes=[
            pltpu.SMEM(random_blocks.shape[::-1], jnp.int32),
            pltpu.VMEM((2, tok, width), jnp.bfloat16),
            pltpu.VMEM((4, shards, length, HD), jnp.bfloat16),
            pltpu.VMEM((uly, 1, BLOCK), jnp.float32),
            pltpu.VMEM((half, uly, 1, BLOCK), jnp.float32),
            pltpu.VMEM((shards, shards * per, length), jnp.float32),
            pltpu.VMEM((2, shards, 3, length), jnp.float32),
            pltpu.VMEM((tiles, length, length), jnp.float32),
            pltpu.VMEM((tiles, length, length), jnp.bfloat16),
            pltpu.VMEM((length, length), jnp.bfloat16),
            pltpu.VMEM((3, shards, length, HD), jnp.float32),
            pltpu.VMEM((shards, length, HD), jnp.float32),
            pltpu.VMEM((3, half, length, HD), jnp.bfloat16),
            dma((1,)),
            dma((4, half, 2)),
            dma((2, shards)),
            dma((2,)),
            dma((shards,)),
            dma((1,)),
            dma((1,)),
            dma((1,)),
            dma((1,)),
            dma((3,)),
        ],
        compiler_params=pltpu.CompilerParams(
            collective_id=0, has_side_effects=True, vmem_limit_bytes=32 * 1024 * 1024
        ),
    )(*placed)
    return pl.pallas_call(
        write_out,
        out_shape=[jax.ShapeDtypeStruct((tok, width), jnp.bfloat16)] * 3,
        in_specs=[vmem],
        out_specs=[hbm] * 3,
        scratch_shapes=[dma((6,))],
        compiler_params=pltpu.CompilerParams(vmem_limit_bytes=32 * 1024 * 1024),
    )(results)


def wide_or_fused(shards, uly, *operands):
    tok, width = operands[0].shape
    length = tok * uly
    fits = shards * length * length * 4 <= 4 * 1024 * 1024
    paired = shards % 4 == 0 and uly % shards == 0
    if fits and paired and width == uly * HD and BLOCK % tok == 0 and length % BLOCK == 0:
        return tuple(fused_on_device(shards, uly, *operands))
    return on_device(*operands)


def solution(mesh):
    return jax.shard_map(
        functools.partial(wide_or_fused, mesh.shape["blk"], mesh.shape["uly"]),
        mesh=mesh,
        in_specs=(
            P(("blk", "uly"), None),
            P(("blk", "uly"), None),
            P(("blk", "uly"), None),
            P(("blk", "uly"), None),
            P(("blk", "uly"), None),
            P(),
        ),
        out_specs=(P(("blk", "uly"), None), P(("blk", "uly"), None), P(("blk", "uly"), None)),
        check_vma=False,
    )
```

```python
import functools
import math

import jax
import jax.numpy as jnp
from jax import lax
from jax.experimental import pallas as pl
from jax.experimental.pallas import tpu as pltpu
from jax.sharding import PartitionSpec as P

HD = 128
BLOCK = 128
RAND = 3
CAP = 2


def named_table(random_blocks, per_shard):
    block_count = random_blocks.shape[0]
    shard_count = block_count // per_shard
    entries = random_blocks.reshape(shard_count, per_shard * RAND)
    block_ids = jnp.arange(block_count, dtype=jnp.int32)
    named = jnp.any(entries[:, :, None] == block_ids[None, None, :], axis=1)
    owner = block_ids // per_shard
    named = named & (owner[None, :] != jnp.arange(shard_count, dtype=jnp.int32)[:, None])
    grouped = named.reshape(shard_count, shard_count, per_shard).astype(jnp.int32)
    rank_in = jnp.cumsum(grouped, axis=2) - grouped
    return (grouped, rank_in)


def send_slots(grouped, rank_in, cycle_rank, per_shard):
    mine = lax.dynamic_index_in_dim(grouped, cycle_rank, 1, keepdims=False)
    mine_rank = lax.dynamic_index_in_dim(rank_in, cycle_rank, 1, keepdims=False)
    slot_ids = jnp.arange(CAP, dtype=jnp.int32)
    hit = (mine[:, None, :] == 1) & (mine_rank[:, None, :] == slot_ids[None, :, None])
    positions = jnp.arange(per_shard, dtype=jnp.int32)
    select = jnp.sum(jnp.where(hit, positions[None, None, :], 0), axis=2)
    filled = jnp.any(hit, axis=2)
    return (select, filled)


def on_device(query_proj, key_proj, value_proj, attn_output, out_grad, random_blocks):
    tok_count = query_proj.shape[0]
    head_count = query_proj.shape[1] // HD
    score_scale = HD ** (-0.5)
    extent = 3 + RAND

    def to_heads(tensor):
        return tensor.reshape(tok_count, head_count, HD)

    query_rows, key_rows, value_rows, output_rows, grad_rows = (
        lax.all_to_all(to_heads(query_proj), "uly", split_axis=1, concat_axis=0, tiled=True),
        lax.all_to_all(to_heads(key_proj), "uly", split_axis=1, concat_axis=0, tiled=True),
        lax.all_to_all(to_heads(value_proj), "uly", split_axis=1, concat_axis=0, tiled=True),
        lax.all_to_all(to_heads(attn_output), "uly", split_axis=1, concat_axis=0, tiled=True),
        lax.all_to_all(to_heads(out_grad), "uly", split_axis=1, concat_axis=0, tiled=True),
    )
    row_delta = jnp.sum(
        output_rows.astype(jnp.float32) * grad_rows.astype(jnp.float32), axis=2
    ).reshape(-1)
    shard_len = query_rows.shape[0]
    per_shard = shard_len // BLOCK
    query_blocks = query_rows.reshape(per_shard, BLOCK, HD)
    key_blocks = key_rows.reshape(per_shard, BLOCK, HD)
    value_blocks = value_rows.reshape(per_shard, BLOCK, HD)
    grad_blocks = grad_rows.reshape(per_shard, BLOCK, HD)
    delta_blocks = row_delta.reshape(per_shard, BLOCK)
    cycle_size = lax.axis_size("blk")
    cycle_rank = lax.axis_index("blk")
    block_count = random_blocks.shape[0]
    grouped, rank_in = named_table(random_blocks, per_shard)
    select, filled = send_slots(grouped, rank_in, cycle_rank, per_shard)
    key_send = jnp.where(
        filled[:, :, None, None],
        jnp.take(key_blocks, select.reshape(-1), axis=0).reshape(cycle_size, CAP, BLOCK, HD),
        jnp.zeros((), jnp.bfloat16),
    )
    value_send = jnp.where(
        filled[:, :, None, None],
        jnp.take(value_blocks, select.reshape(-1), axis=0).reshape(cycle_size, CAP, BLOCK, HD),
        jnp.zeros((), jnp.bfloat16),
    )
    extra_key = jnp.broadcast_to(
        jnp.stack([key_blocks[per_shard - 1], key_blocks[0]])[None], (cycle_size, 2, BLOCK, HD)
    )
    extra_value = jnp.broadcast_to(
        jnp.stack([value_blocks[per_shard - 1], value_blocks[0]])[None], (cycle_size, 2, BLOCK, HD)
    )
    all_key, all_value = (
        lax.all_to_all(
            jnp.concatenate([key_send, extra_key], axis=1),
            "blk",
            split_axis=0,
            concat_axis=0,
            tiled=True,
        ),
        lax.all_to_all(
            jnp.concatenate([value_send, extra_value], axis=1),
            "blk",
            split_axis=0,
            concat_axis=0,
            tiled=True,
        ),
    )
    far_key = all_key[:, :CAP]
    far_value = all_value[:, :CAP]
    before_rank = jnp.maximum(cycle_rank - 1, 0)
    prev_key = lax.dynamic_index_in_dim(all_key, before_rank, 0, keepdims=False)[CAP]
    prev_value = lax.dynamic_index_in_dim(all_value, before_rank, 0, keepdims=False)[CAP]
    first_key = all_key[0, CAP + 1]
    first_value = all_value[0, CAP + 1]
    key_store = jnp.concatenate(
        [key_blocks, prev_key[None], first_key[None], far_key.reshape(cycle_size * CAP, BLOCK, HD)],
        axis=0,
    )
    value_store = jnp.concatenate(
        [
            value_blocks,
            prev_value[None],
            first_value[None],
            far_value.reshape(cycle_size * CAP, BLOCK, HD),
        ],
        axis=0,
    )
    store_size = key_store.shape[0]
    picked = lax.dynamic_slice_in_dim(random_blocks, cycle_rank * per_shard, per_shard, 0)
    own_rank = lax.dynamic_index_in_dim(rank_in, cycle_rank, 0, keepdims=False).reshape(-1)
    all_ids = jnp.arange(block_count, dtype=jnp.int32)
    slot_of = jnp.sum(
        jnp.where(picked[:, :, None] == all_ids[None, None, :], own_rank[None, None, :], 0), axis=2
    )
    owner = picked // per_shard
    random_index = jnp.where(
        owner == cycle_rank, picked - cycle_rank * per_shard, per_shard + 2 + owner * CAP + slot_of
    )
    local_ids = jnp.arange(per_shard, dtype=jnp.int32)
    global_ids = cycle_rank * per_shard + local_ids
    listed = jnp.concatenate(
        [
            global_ids[:, None],
            global_ids[:, None] - 1,
            jnp.zeros((per_shard, 1), jnp.int32),
            picked,
        ],
        axis=1,
    )
    first_index = jnp.zeros((per_shard, 1), jnp.int32) + jnp.where(
        cycle_rank == 0, 0, per_shard + 1
    ).astype(jnp.int32)
    store_index = jnp.concatenate(
        [
            local_ids[:, None],
            jnp.where(local_ids >= 1, local_ids - 1, per_shard)[:, None],
            first_index,
            random_index,
        ],
        axis=1,
    )
    order = jnp.arange(extent, dtype=jnp.int32)
    earlier = order[None, :] < order[:, None]
    repeated = jnp.any((listed[:, :, None] == listed[:, None, :]) & earlier[None, :, :], axis=2)
    usable = (listed >= 0) & jnp.logical_not(repeated)
    within = jnp.arange(BLOCK, dtype=jnp.int32)
    group = math.gcd(per_shard, max(1, 512 // BLOCK))
    group_count = per_shard // group

    def group_turn(carry, group_index):
        key_grad_store, value_grad_store = carry
        first = group_index * group
        query_grp = lax.dynamic_slice_in_dim(query_blocks, first, group, 0)
        grad_grp = lax.dynamic_slice_in_dim(grad_blocks, first, group, 0)
        delta_grp = lax.dynamic_slice_in_dim(delta_blocks, first, group, 0)
        index_grp = lax.dynamic_slice_in_dim(store_index, first, group, 0).reshape(-1)
        listed_grp = lax.dynamic_slice_in_dim(listed, first, group, 0)
        usable_grp = lax.dynamic_slice_in_dim(usable, first, group, 0)
        key_sel = jnp.take(key_store, index_grp, axis=0).reshape(group, extent * BLOCK, HD)
        value_sel = jnp.take(value_store, index_grp, axis=0).reshape(group, extent * BLOCK, HD)
        scores = (
            jnp.einsum("gqd,gkd->gqk", query_grp, key_sel, preferred_element_type=jnp.float32)
            * score_scale
        )
        query_pos = (cycle_rank * per_shard + first + jnp.arange(group, dtype=jnp.int32))[
            :, None
        ] * BLOCK + within[None, :]
        key_pos = (listed_grp[:, :, None] * BLOCK + within[None, None, :]).reshape(
            group, extent * BLOCK
        )
        allowed = jnp.repeat(usable_grp, BLOCK, axis=1)[:, None, :] & (
            key_pos[:, None, :] <= query_pos[:, :, None]
        )
        row_max = jnp.max(jnp.where(allowed, scores, -1e30), axis=2)
        total = jnp.sum(jnp.where(allowed, jnp.exp(scores - row_max[:, :, None]), 0.0), axis=2)
        log_total = row_max + jnp.log(total)
        probs = jnp.where(allowed, jnp.exp(scores - log_total[:, :, None]), 0.0)
        prob_grad = jnp.einsum(
            "gqd,gkd->gqk", grad_grp, value_sel, preferred_element_type=jnp.float32
        )
        score_grad = (probs * (prob_grad - delta_grp[:, :, None]) * score_scale).astype(
            jnp.bfloat16
        )
        query_part = jnp.einsum(
            "gqk,gkd->gqd", score_grad, key_sel, preferred_element_type=jnp.float32
        ).astype(jnp.bfloat16)
        key_part = jnp.einsum(
            "gqk,gqd->gkd", score_grad, query_grp, preferred_element_type=jnp.float32
        )
        value_part = jnp.einsum(
            "gqk,gqd->gkd", probs.astype(jnp.bfloat16), grad_grp, preferred_element_type=jnp.float32
        )
        key_grad_store = key_grad_store.at[index_grp].add(
            key_part.reshape(group * extent, BLOCK, HD)
        )
        value_grad_store = value_grad_store.at[index_grp].add(
            value_part.reshape(group * extent, BLOCK, HD)
        )
        return ((key_grad_store, value_grad_store), query_part)

    zero_store = jnp.zeros((store_size, BLOCK, HD), jnp.float32)
    (key_grad_store, value_grad_store), query_parts = lax.scan(
        group_turn, (zero_store, zero_store), jnp.arange(group_count, dtype=jnp.int32)
    )
    query_acc = query_parts.reshape(shard_len, HD)
    key_acc = key_grad_store[:per_shard]
    value_acc = value_grad_store[:per_shard]
    far_key_grad = key_grad_store[per_shard + 2 :].reshape(cycle_size, CAP, BLOCK, HD)
    far_value_grad = value_grad_store[per_shard + 2 :].reshape(cycle_size, CAP, BLOCK, HD)
    dest_ids = jnp.arange(cycle_size, dtype=jnp.int32)
    to_prev = (dest_ids == cycle_rank - 1)[:, None, None]
    to_first = (dest_ids == 0)[:, None, None]
    extra_key_grad = jnp.stack(
        [
            jnp.where(to_prev, key_grad_store[per_shard][None], 0.0),
            jnp.where(to_first, key_grad_store[per_shard + 1][None], 0.0),
        ],
        axis=1,
    )
    extra_value_grad = jnp.stack(
        [
            jnp.where(to_prev, value_grad_store[per_shard][None], 0.0),
            jnp.where(to_first, value_grad_store[per_shard + 1][None], 0.0),
        ],
        axis=1,
    )
    all_key_back, all_value_back = (
        lax.all_to_all(
            jnp.concatenate([far_key_grad, extra_key_grad], axis=1),
            "blk",
            split_axis=0,
            concat_axis=0,
            tiled=True,
        ),
        lax.all_to_all(
            jnp.concatenate([far_value_grad, extra_value_grad], axis=1),
            "blk",
            split_axis=0,
            concat_axis=0,
            tiled=True,
        ),
    )
    back_key = all_key_back[:, :CAP]
    back_value = all_value_back[:, :CAP]
    prev_back = jnp.stack(
        [jnp.sum(all_key_back[:, CAP], axis=0), jnp.sum(all_value_back[:, CAP], axis=0)]
    )
    first_back = jnp.stack(
        [jnp.sum(all_key_back[:, CAP + 1], axis=0), jnp.sum(all_value_back[:, CAP + 1], axis=0)]
    )
    key_acc = key_acc.at[per_shard - 1].add(prev_back[0]).at[0].add(first_back[0])
    value_acc = value_acc.at[per_shard - 1].add(prev_back[1]).at[0].add(first_back[1])
    back_key = jnp.where(filled[:, :, None, None], back_key, 0.0).reshape(
        cycle_size * CAP, BLOCK, HD
    )
    back_value = jnp.where(filled[:, :, None, None], back_value, 0.0).reshape(
        cycle_size * CAP, BLOCK, HD
    )
    key_acc = key_acc.at[select.reshape(-1)].add(back_key).reshape(shard_len, HD)
    value_acc = value_acc.at[select.reshape(-1)].add(back_value).reshape(shard_len, HD)
    outgoing = (
        query_acc.reshape(shard_len, 1, HD),
        key_acc.astype(jnp.bfloat16).reshape(shard_len, 1, HD),
        value_acc.astype(jnp.bfloat16).reshape(shard_len, 1, HD),
    )
    query_back, key_back, value_back = (
        lax.all_to_all(outgoing[0], "uly", split_axis=0, concat_axis=1, tiled=True),
        lax.all_to_all(outgoing[1], "uly", split_axis=0, concat_axis=1, tiled=True),
        lax.all_to_all(outgoing[2], "uly", split_axis=0, concat_axis=1, tiled=True),
    )
    return (
        query_back.reshape(tok_count, head_count * HD),
        key_back.reshape(tok_count, head_count * HD),
        value_back.reshape(tok_count, head_count * HD),
    )


NEG = -1e30
KEY, QUERY, GRAD, VALUE = 0, 1, 2, 3
D_QUERY, D_KEY, D_VALUE = 0, 1, 2
ROWS_BY_COLS = (((1,), (1,)), ((), ()))
COLS_BY_COLS = (((0,), (0,)), ((), ()))


FIRST_TILES = ((0, 0), (1, 0), (2, 0), (3, 0), (3, 3), (3, 2), (3, 1), (2, 2), (1, 1), (2, 1))


def flip(value, mask, count):
    if count & (count - 1):
        return lax.rem(value + mask, count)
    for bit in range(count.bit_length() - 1):
        if mask >> bit & 1:
            value = value + (1 << bit) * (1 - 2 * (value // (1 << bit) % 2))
    return value


def core_of(shard):
    return (shard + 1) // 2 % 2


def fused_kernel(
    shards,
    uly,
    picks_hbm,
    q_ref,
    k_ref,
    v_ref,
    o_ref,
    g_ref,
    out_ref,
    picks_ref,
    rows_in,
    held,
    delta_send,
    delta_recv,
    bias,
    stats,
    scores,
    probs_low,
    score_grads,
    acc,
    partial,
    outgoing,
    zs,
    zr,
    sb,
    st,
    pt,
    ds_sem,
    dr_sem,
    os_sem,
    or_sem,
    il,
):
    tok = q_ref.shape[0]
    length = tok * uly
    per = length // BLOCK
    gp = BLOCK // tok
    blocks = per * shards
    planes = uly // shards
    base = (uly // 2 - planes) // 2
    scale = HD ** (-0.5)
    f32 = jnp.float32
    b = lax.axis_index("blk")
    u = lax.axis_index("uly")
    uz, core = u // 2, u % 2
    plane = uz - base
    is_home = jnp.logical_and(plane >= 0, plane < planes)
    near = jnp.clip(plane, 0, planes - 1)
    head = b + shards * near
    own_source = jnp.logical_and(is_home, core_of(b) == core)
    inputs = {KEY: k_ref, QUERY: q_ref, VALUE: v_ref, GRAD: g_ref}
    mesh_ids = pl.DeviceIdType.MESH

    def home(h, s):
        return h % shards, (base + h // shards) * 2 + core_of(s)

    sibling = (b, uz * 2 + 1 - core)

    def is_self(place):
        return jnp.logical_and(place[0] == b, place[1] == u)

    def ids(place):
        return {"blk": place[0], "uly": place[1]}

    def cols(p):
        return pl.ds(pl.multiple_of(p * HD, HD), HD)

    def rows(p):
        return pl.ds(pl.multiple_of(p * tok, tok), tok)

    def remote(source, target, send, recv, place):
        return pltpu.make_async_remote_copy(
            src_ref=source,
            dst_ref=target,
            send_sem=send,
            recv_sem=recv,
            device_id=ids(place),
            device_id_type=mesh_ids,
        )

    def ship(source, target, send, recv, place, maybe_here):
        if not maybe_here:
            remote(source, target, send, recv, place).start()
            return
        mine = is_self(place)

        @pl.when(jnp.logical_not(mine))
        def _():
            remote(source, target, send, recv, place).start()

        @pl.when(mine)
        def _():
            pltpu.make_async_copy(source, target, recv).start()

    def heads():
        return [(flip(head, mask, uly), mask == 0) for mask in reversed(range(uly))]

    def z_send(t):
        for h, maybe_here in heads():
            ship(
                inputs[t].at[:, cols(h)],
                held.at[t, b, rows(u), :],
                zs.at[0],
                zr.at[t, b // 2, u // (uly // 2)],
                home(h, b),
                maybe_here,
            )

    fetches = (
        pltpu.make_async_copy(o_ref, rows_in.at[0], il.at[0]),
        pltpu.make_async_copy(g_ref, rows_in.at[1], il.at[1]),
        pltpu.make_async_copy(picks_hbm, picks_ref, il.at[2]),
    )
    barrier = pltpu.get_barrier_semaphore()

    def greet(place):
        pl.semaphore_signal(barrier, inc=1, device_id=ids(place), device_id_type=mesh_ids)

    with jax.named_scope("greet"):

        @pl.when(is_home)
        def _():
            for p in range(uly):
                for j in range(shards // 2):
                    place = (2 * j + (core + j) % 2, p)
                    pl.when(jnp.logical_not(is_self(place)))(functools.partial(greet, place))
            greet(sibling)

        for fetch in fetches:
            fetch.start()
    with jax.named_scope("barrier"):
        pl.semaphore_wait(
            barrier, uly - jnp.where(own_source, 1, 0) + jnp.where(is_home, 1, 0)
        )
    with jax.named_scope("send_kq"):
        z_send(KEY)
        z_send(QUERY)

    with jax.named_scope("prep"):
        for fetch in fetches:
            fetch.wait()
        product = rows_in[0].astype(f32) * rows_in[1].astype(f32)
        high = product.astype(jnp.bfloat16)
        low = (product - high.astype(f32)).astype(jnp.bfloat16)
        head_of = lax.broadcasted_iota(jnp.int32, (uly, uly * HD), 1) // HD
        pick_head = jnp.where(
            head_of == lax.broadcasted_iota(jnp.int32, (uly, uly * HD), 0), 1.0, 0.0
        ).astype(jnp.bfloat16)
        sums = sum(
            lax.dot_general(
                pick_head,
                jnp.concatenate([part] * gp, axis=0),
                ROWS_BY_COLS,
                preferred_element_type=f32,
            )
            for part in (high, low)
        )
        place_of = lax.broadcasted_iota(jnp.int32, (uly, BLOCK), 1) // tok
        sums = jnp.where(place_of == lax.rem(u, gp), sums, 0.0)
        for h in range(uly):
            delta_send[h] = sums[h : h + 1]

    with jax.named_scope("send_gv"):
        for h, maybe_here in heads():
            ship(
                delta_send.at[h],
                delta_recv.at[b // 2, u],
                ds_sem.at[0],
                dr_sem.at[0],
                home(h, b),
                maybe_here,
            )
        z_send(GRAD)
        z_send(VALUE)

    def at(jb):
        return pl.ds(jb * BLOCK, BLOCK)

    def run_home(c):
        owned = [s for s in range(shards) if core_of(s) == c]
        foreign = [s for s in range(shards) if core_of(s) != c and s > owned[0]]
        lent = [s for s in owned if any(core_of(k) != c and k < s for k in range(shards))]
        tiles = [(q, k) for k in owned for q in range(k, shards)]
        slot = {tile: n for n, tile in enumerate(tiles)}
        q_all = sorted({q for q, _ in tiles})
        q_own = [q for q in q_all if q in owned]
        q_far = [q for q in q_all if q not in owned]
        pair_of = {QUERY: 0, GRAD: 1}
        wide = length // 2

        def own(t):
            with jax.named_scope(f"own_{t}"):
                for i in range(2):
                    n = lax.rem(u // (uly // 2) + i, 2)
                    for s in lent + [s for s in owned if s not in lent]:
                        ref = held.at[t, s, pl.ds(pl.multiple_of(n * wide, wide), wide), :]
                        remote(ref, ref, zs.at[0], zr.at[t, s // 2, n], (b, u)).wait_recv()
                        if t in pair_of and s in lent:
                            sem = sb.at[pair_of[t], s]
                            remote(ref, ref, sem, sem, sibling).start()

        def lent_copy(t, s):
            sem = sb.at[pair_of[t], s]
            return remote(held.at[t, s], held.at[t, s], sem, sem, sibling)

        turn = math.log2(math.e) * scale

        def keys_for(q, k, a):
            return (a + 1) * wide if q == k else length

        def first_lane(q, k, r):
            return r * wide if q == k else 0

        def lanes(a):
            return pl.ds(a * wide, wide)

        def fold(tile, op):
            return op(tile.reshape(tile.shape[0] // 8, 8, tile.shape[1]), axis=0)

        def bias_row(q, k, n, a):
            return bias[q, pl.ds(k * per + n, 1), lanes(a)]

        def make_scores(q, k, tops):
            new = []
            with jax.named_scope(f"scores_{q}_{k}"):
                for a in range(2):
                    count = keys_for(q, k, a)
                    tile = lax.dot_general(
                        held[KEY, k, :count, :],
                        held[QUERY, q, lanes(a), :],
                        ROWS_BY_COLS,
                        preferred_element_type=f32,
                    )
                    if q == k:
                        key_at = lax.broadcasted_iota(jnp.int32, (wide, wide), 0)
                        query_at = lax.broadcasted_iota(jnp.int32, (wide, wide), 1)
                        last = jnp.where(key_at <= query_at, tile[a * wide :], NEG)
                        tile = jnp.concatenate([tile[: a * wide], last], axis=0) if a else last
                    scores[slot[q, k], :count, lanes(a)] = tile
                    top = tops[a] if tops else None
                    for n in range(count // BLOCK):
                        part = fold(tile[n * BLOCK : (n + 1) * BLOCK], jnp.max)
                        part = part * turn + bias_row(q, k, n, a)
                        top = part if top is None else jnp.maximum(top, part)
                    new.append(top)
            return new

        def make_exps(q, tops):
            totals = []
            with jax.named_scope(f"exps_{q}"):
                for a in range(2):
                    top = jnp.maximum(jnp.max(tops[a], axis=0, keepdims=True), 0.1 * NEG)
                    total = jnp.zeros((8, wide), f32)
                    for k in owned:
                        if k > q:
                            continue
                        for n in range(keys_for(q, k, a) // BLOCK):
                            shift = top - bias_row(q, k, n, a)
                            tile = scores[slot[q, k], at(n), lanes(a)]
                            tile = jnp.exp2(tile * turn - shift)
                            scores[slot[q, k], at(n), lanes(a)] = tile
                            total = total + fold(tile, jnp.sum)
                    total = jnp.sum(total, axis=0, keepdims=True)
                    if q in lent or q in q_far:
                        stats[c, q, 0:1, lanes(a)] = top
                        stats[c, q, 1:2, lanes(a)] = total
                    totals.append(total)
            return jnp.concatenate(totals, axis=1)

        def pieces_of(q, k, start, stop):
            if q == k and start < wide < stop:
                return ((start, wide, 0), (wide, stop, wide))
            return ((start, stop, wide if q == k and start >= wide else 0),)

        def make_probs(q, k, start, stop, factor):
            with jax.named_scope(f"probs_{q}_{k}"):
                for low, high, first in pieces_of(q, k, start, stop):
                    probs = scores[slot[q, k], low:high, first:] * factor[:, first:]
                    probs_low[slot[q, k], low:high, first:] = probs.astype(jnp.bfloat16)

        def add(ref, value, fresh, result=None):
            if not fresh:
                value = value + ref[...]
            if result is None:
                ref[...] = value
            else:
                result[...] = value.astype(jnp.bfloat16)

        def make_values(q, k, start, stop, fresh, last):
            with jax.named_scope(f"values_{q}_{k}"):
                for low, high, first in pieces_of(q, k, start, stop):
                    product = jnp.dot(
                        probs_low[slot[q, k], low:high, first:],
                        held[GRAD, q, first:, :],
                        preferred_element_type=f32,
                    )
                    result = outgoing.at[D_VALUE, k // 2, low:high, :] if last else None
                    add(acc.at[D_VALUE, k, low:high, :], product, fresh, result)

        def make_grads(q, k, factor, delta):
            with jax.named_scope(f"grads_{q}_{k}"):
                for a in range(2):
                    count = keys_for(q, k, a)
                    prob_grad = lax.dot_general(
                        held[VALUE, k, :count, :],
                        held[GRAD, q, lanes(a), :],
                        ROWS_BY_COLS,
                        preferred_element_type=f32,
                    )
                    span = slice(a * wide, (a + 1) * wide)
                    grads = (scores[slot[q, k], :count, lanes(a)] * factor[:, span]) * (
                        prob_grad - delta[:, span]
                    )
                    score_grads[:count, lanes(a)] = grads.astype(jnp.bfloat16)

        def add_query(q, k, a, fresh, last):
            count = keys_for(q, k, a)
            product = lax.dot_general(
                score_grads[:count, lanes(a)],
                held[KEY, k, :count, :],
                COLS_BY_COLS,
                preferred_element_type=f32,
            )
            result = outgoing.at[D_QUERY, q // 2, lanes(a), :] if last else None
            add(acc.at[D_QUERY, q, lanes(a), :], product, fresh, result)

        def add_key(q, k, r, fresh, last):
            first = first_lane(q, k, r)
            product = jnp.dot(
                score_grads[lanes(r), first:],
                held[QUERY, q, first:, :],
                preferred_element_type=f32,
            )
            result = outgoing.at[D_KEY, k // 2, lanes(r), :] if last else None
            add(acc.at[D_KEY, k, lanes(r), :], product, fresh, result)

        def send_result(t, s, start=0, stop=length):
            with jax.named_scope(f"send_{t}_{s}_{start}"):
                inner, outer = 2 * base, 2 * (base + planes)
                targets = [(p, False) for p in range(uly) if not inner <= p < outer]
                for mask in reversed(range(outer - inner)):
                    p = inner + flip(u - inner, mask, outer - inner)
                    targets.append((p, mask == 0))
                for p, maybe_here in targets[start // tok : stop // tok]:
                    ship(
                        outgoing.at[t, s // 2, rows(p), :],
                        out_ref.at[t, :, cols(head)],
                        os_sem.at[0],
                        or_sem.at[0],
                        (s, p),
                        maybe_here,
                    )

        own(KEY)
        own(QUERY)
        tops, totals = {}, {}

        def all_scores(queries):
            for q in queries:
                for k in owned:
                    if k <= q:
                        tops[q] = make_scores(q, k, tops.get(q))
            for q in queries:
                totals[q] = make_exps(q, tops[q])

        all_scores(lent if c else [])
        with jax.named_scope("lent_q"):
            for q in q_far:
                lent_copy(QUERY, q).wait_recv()
        all_scores(q_far if c else lent + q_far)
        with jax.named_scope("stats"):
            remote(delta_recv, delta_recv, ds_sem.at[0], dr_sem.at[0], (b, u)).wait_recv()
            for s in owned:
                pieces = []
                for n in range(per):
                    piece = delta_recv[s // 2, n * gp]
                    for i in range(1, gp):
                        piece = piece + delta_recv[s // 2, n * gp + i]
                    pieces.append(piece)
                stats[c, s, 2:3, :] = jnp.concatenate(pieces, axis=1)
            remote(stats.at[c], stats.at[c], st.at[c], st.at[c], sibling).start()
        all_scores([q for q in q_own if q not in lent])
        own(GRAD)
        with jax.named_scope("stats_wait"):
            remote(stats.at[1 - c], stats.at[1 - c], st.at[c], st.at[1 - c], sibling).wait_recv()
        factors, deltas = {}, {}
        for q in q_all:
            if q in lent or q in q_far:
                top, total = stats[c, q, 0:1, :], stats[c, q, 1:2, :]
                top_far, total_far = stats[1 - c, q, 0:1, :], stats[1 - c, q, 1:2, :]
                high = jnp.maximum(top, top_far)
                share = jnp.exp2(top - high)
                factors[q] = share / (share * total + jnp.exp2(top_far - high) * total_far)
            else:
                factors[q] = 1.0 / totals[q]
            deltas[q] = stats[c if q in owned else 1 - c, q, 2:3, :]
        started = set()

        def starts(*what):
            new = what not in started
            started.add(what)
            return new

        have = set(q_own)
        early = min(tok * 2 * base, wide) if c == core_of(0) else 0
        spans = [(0, early), (early, length)] if early else [(0, length)]
        for start, stop in spans:
            for k in owned:
                queries = [q for q in q_own + q_far if q >= k]
                for q in queries:
                    make_probs(q, k, start, stop, factors[q])
                    if q not in have:
                        with jax.named_scope("lent_g"):
                            lent_copy(GRAD, q).wait_recv()
                        have.add(q)
                    make_values(q, k, start, stop, q == queries[0], q == queries[-1])
                send_result(D_VALUE, k, start, stop)
        own(VALUE)
        todo = [tile for tile in FIRST_TILES if tile in tiles]
        todo += [tile for tile in tiles if tile not in todo]
        waiting = []

        def finish_queries():
            while waiting:
                q = waiting.pop(0)
                with jax.named_scope(f"partial_{q}"):
                    ref = partial.at[q]
                    remote(ref, ref, pt.at[q], pt.at[q], sibling).wait_recv()
                    total = acc[D_QUERY, q] + partial[q]
                    outgoing[D_QUERY, q // 2] = total.astype(jnp.bfloat16)
                send_result(D_QUERY, q)

        while todo:
            q, k = todo.pop(0)
            make_grads(q, k, factors[q] * scale, deltas[q])
            fresh_query, fresh_key = starts("q", q), starts("k", k)
            last_query = all(tile[0] != q for tile in todo)
            last_key = all(tile[1] != k for tile in todo)
            whole_query = last_query and q in q_own and q not in lent
            with jax.named_scope(f"dots_{q}_{k}"):
                for a in range(2):
                    add_query(q, k, a, fresh_query, whole_query)
                for r in range(2):
                    add_key(q, k, r, fresh_key, last_key)
            finish_queries()
            if last_query:
                if q in q_far:
                    ref = acc.at[D_QUERY, q]
                    remote(ref, partial.at[q], pt.at[q], pt.at[q], sibling).start()
                elif q in lent:
                    waiting.append(q)
                else:
                    send_result(D_QUERY, q)
            if last_key:
                send_result(D_KEY, k)
        finish_queries()
        with jax.named_scope("lent_sent"):
            for s in lent:
                for t in pair_of:
                    lent_copy(t, s).wait_send()
            for q in q_far:
                ref = acc.at[D_QUERY, q]
                remote(ref, ref, pt.at[q], pt.at[q], sibling).wait_send()
            remote(stats.at[c], stats.at[c], st.at[c], st.at[c], sibling).wait_send()

    @pl.when(is_home)
    def _():
        with jax.named_scope("bias"):
            lane_block = lax.broadcasted_iota(jnp.int32, (1, length), 1) // BLOCK
            key_block = lax.broadcasted_iota(jnp.int32, (blocks, length), 0)
            for s in range(shards):
                query_block = lane_block + s * per
                hit = (key_block == query_block) | (key_block == query_block - 1)
                hit = hit | (key_block == 0)
                for r in range(RAND):
                    named = jnp.zeros((1, length), jnp.int32)
                    for i in range(per):
                        named = jnp.where(lane_block == i, picks_ref[r, s * per + i], named)
                    hit = hit | (key_block == named)
                hit = hit & (key_block <= query_block)
                bias[s] = jnp.where(hit, 0.0, NEG)
        for c in range(2):
            pl.when(core == c)(functools.partial(run_home, c))

    def drain(count):
        ref = held.at[:, 0, pl.ds(0, count * tok), :]
        remote(ref, ref, zs.at[0], zr.at[0, 0, 0], (b, u)).wait_send()
        ref = delta_send.at[pl.ds(0, count)]
        remote(ref, ref, ds_sem.at[0], dr_sem.at[0], (b, u)).wait_send()

    with jax.named_scope("sent"):
        pl.when(own_source)(lambda: drain(uly - 1))
        pl.when(jnp.logical_not(own_source))(lambda: drain(uly))

        @pl.when(own_source)
        def _():
            ref = outgoing.at[:, :, pl.ds(0, length - tok // (shards // 2)), :]
            remote(ref, ref, os_sem.at[0], or_sem.at[0], (b, u)).wait_send()

        @pl.when(jnp.logical_and(is_home, jnp.logical_not(own_source)))
        def _():
            remote(outgoing, outgoing, os_sem.at[0], or_sem.at[0], (b, u)).wait_send()

    with jax.named_scope("landed"):
        remote(out_ref, out_ref, os_sem.at[0], or_sem.at[0], (b, u)).wait_recv()


def write_out(held, a_out, b_out, c_out, done):
    half = held.shape[1] // 2
    writes = [
        pltpu.make_async_copy(
            held.at[i, pl.ds(n * half, half)], target.at[pl.ds(n * half, half)], done.at[2 * i + n]
        )
        for i, target in enumerate((a_out, b_out, c_out))
        for n in range(2)
    ]
    for write in writes:
        write.start()
    for write in writes:
        write.wait()


def fused_on_device(shards, uly, q, k, v, o, g, random_blocks):
    tok, width = q.shape
    length = tok * uly
    per = length // BLOCK
    half = shards // 2
    tiles = max(
        sum(shards - k for k in range(shards) if core_of(k) == core) for core in range(2)
    )
    dma = pltpu.SemaphoreType.DMA
    hbm = pl.BlockSpec(memory_space=pltpu.HBM)
    vmem = pl.BlockSpec(memory_space=pltpu.VMEM)
    placed = [
        pltpu.with_memory_space_constraint(x, pltpu.HBM) for x in (random_blocks.T, q, k, v, o, g)
    ]
    results = pl.pallas_call(
        functools.partial(fused_kernel, shards, uly),
        out_shape=jax.ShapeDtypeStruct((3, tok, width), jnp.bfloat16),
        in_specs=[hbm] * 6,
        out_specs=vmem,
        scratch_shapes=[
            pltpu.SMEM(random_blocks.shape[::-1], jnp.int32),
            pltpu.VMEM((2, tok, width), jnp.bfloat16),
            pltpu.VMEM((4, shards, length, HD), jnp.bfloat16),
            pltpu.VMEM((uly, 1, BLOCK), jnp.float32),
            pltpu.VMEM((half, uly, 1, BLOCK), jnp.float32),
            pltpu.VMEM((shards, shards * per, length), jnp.float32),
            pltpu.VMEM((2, shards, 3, length), jnp.float32),
            pltpu.VMEM((tiles, length, length), jnp.float32),
            pltpu.VMEM((tiles, length, length), jnp.bfloat16),
            pltpu.VMEM((length, length), jnp.bfloat16),
            pltpu.VMEM((3, shards, length, HD), jnp.float32),
            pltpu.VMEM((shards, length, HD), jnp.float32),
            pltpu.VMEM((3, half, length, HD), jnp.bfloat16),
            dma((1,)),
            dma((4, half, 2)),
            dma((2, shards)),
            dma((2,)),
            dma((shards,)),
            dma((1,)),
            dma((1,)),
            dma((1,)),
            dma((1,)),
            dma((3,)),
        ],
        compiler_params=pltpu.CompilerParams(
            collective_id=0, has_side_effects=True, vmem_limit_bytes=32 * 1024 * 1024
        ),
    )(*placed)
    return pl.pallas_call(
        write_out,
        out_shape=[jax.ShapeDtypeStruct((tok, width), jnp.bfloat16)] * 3,
        in_specs=[vmem],
        out_specs=[hbm] * 3,
        scratch_shapes=[dma((6,))],
        compiler_params=pltpu.CompilerParams(vmem_limit_bytes=32 * 1024 * 1024),
    )(results)


def wide_or_fused(shards, uly, *operands):
    tok, width = operands[0].shape
    length = tok * uly
    fits = shards * length * length * 4 <= 4 * 1024 * 1024
    paired = shards % 4 == 0 and uly % shards == 0
    if fits and paired and width == uly * HD and BLOCK % tok == 0 and length % BLOCK == 0:
        return tuple(fused_on_device(shards, uly, *operands))
    return on_device(*operands)


def solution(mesh):
    return jax.shard_map(
        functools.partial(wide_or_fused, mesh.shape["blk"], mesh.shape["uly"]),
        mesh=mesh,
        in_specs=(
            P(("blk", "uly"), None),
            P(("blk", "uly"), None),
            P(("blk", "uly"), None),
            P(("blk", "uly"), None),
            P(("blk", "uly"), None),
            P(),
        ),
        out_specs=(P(("blk", "uly"), None), P(("blk", "uly"), None), P(("blk", "uly"), None)),
        check_vma=False,
    )
```
